32 devices in a mesh: src: 4 (over y, x), space: 8 (over z, core).
Axes of the slice: x: 2, y: 2, z: 4, core: 2. Of those that a mesh axis runs over, the one named last changes fastest.
Arguments:
- contrast: float32 [2, 64, 256, 256], P(None, None, 'space'), may hold values from -0.4 to 0.45
- measured: float32 [4, 2, 256, 256], P('src', None, 'space'), may hold values from -7 to 7
- positions: int32 [4, 2], P('src'), may hold values from 0 to 255
Outputs:
- contrast_sources: float32 [4, 2, 64, 256, 256], P('src', None, None, 'space')
- contrast_new: float32 [2, 64, 256, 256], P(None, None, 'space')
The draws below stay inside these ranges and needn't reach their ends.
All inputs are finite; a program needn't handle non-finite values.
Results may differ from the reference program's by a relative error of at most 0.0003.
Values sent between devices are 32-bit elements; how exact they have to be, the bound alone decides.
No kernel may reach another device: no remote copies, remote signals or barrier semaphores. Data moves between devices by JAX's collectives and lax.ppermute only.
A program may use at most 128 MiB of HBM per device.

```python
import math
import jax
import jax.numpy as jnp
from jax import lax

NX = 256
NY = 256
NZ = 64
OUTER = 2
SRCS = 4


def draw_contrast(key, part):
    key_real, key_imag = jax.random.split(jax.random.fold_in(key, 11))
    across = jnp.arange(NX).astype(jnp.float32)
    growth = jnp.sqrt(1.0 + 2.0 * across / (NX - 1))[None, :, None]
    shape = (NZ, NX, NY)
    real_part = growth * jax.random.uniform(key_real, shape, jnp.float32, -0.2, 0.25)
    imag_part = growth * jax.random.uniform(key_imag, shape, jnp.float32, -0.02, 0.07)
    return jnp.stack([real_part, imag_part], axis=0)


def draw_measured(key, part):
    shape = (SRCS, 2, NX, NY)
    across = jnp.arange(NX).astype(jnp.float32)
    growth = jnp.sqrt(1.0 + 2.0 * across / (NX - 1))[None, None, :, None]
    values = jnp.clip(jax.random.normal(jax.random.fold_in(key, 23), shape, jnp.float32), -4.0, 4.0)
    return values * growth


def set_ends(values, own_key, low, high):
    shape = values.shape
    spot = [jax.random.randint(jax.random.fold_in(own_key, axis), (), 0, shape[axis]) for axis in range(len(shape))]
    values = values.at[tuple(spot)].set(low)
    longest = shape.index(max(shape))
    spot[longest] = (spot[longest] + 1) % shape[longest]
    return values.at[tuple(spot)].set(high)


def setup_inputs(seed: int = 0) -> dict:
    splits = jax.random.split(jax.random.key(seed), 4)
    contrast = draw_contrast(jax.random.fold_in(splits[3], 71), 0)
    measured = draw_measured(jax.random.fold_in(splits[3], 71), 0)
    positions = set_ends(jax.random.randint(splits[2], (SRCS, 2), 0, NX), jax.random.fold_in(splits[2], 1), 0, NX - 1).astype(jnp.int32)
    return {"contrast": contrast, "measured": measured, "positions": positions}


WAVENUMBER = 2.0 * math.pi / 6.0
DAMPING = 0.3
SOURCE_GAP = 8.0
FLOOR_SHARE = 0.75
REAL_LOW = -0.25
REAL_HIGH = 0.35
IMAG_HIGH = 0.1

def laplace_modes(start_mode, length, total):
    mode_index = (start_mode + jnp.arange(length)).astype(jnp.float32)
    half_sine = jnp.sin(math.pi * mode_index / total)
    return 4.0 * half_sine * half_sine

def green_spectrum(depth_modes, first_modes, second_modes):
    eigen = depth_modes[:, None, None] + first_modes[None, :, None] + second_modes[None, None, :]
    wave_sq = WAVENUMBER * WAVENUMBER
    real_den = eigen - wave_sq
    imag_den = wave_sq * DAMPING
    factor = wave_sq / (real_den * real_den + imag_den * imag_den)
    return (factor * real_den, factor * imag_den)

def incident(positions, start_row, row_count):
    heights = jnp.arange(NZ).astype(jnp.float32) + SOURCE_GAP
    across = (start_row + jnp.arange(row_count)).astype(jnp.float32)
    along_y = jnp.arange(NY).astype(jnp.float32)
    source_x = positions[:, 0].astype(jnp.float32)
    source_y = positions[:, 1].astype(jnp.float32)
    offset_x = across[None, :] - source_x[:, None]
    offset_y = along_y[None, :] - source_y[:, None]
    dist_sq = heights[None, :, None, None] * heights[None, :, None, None] + offset_x[:, None, :, None] * offset_x[:, None, :, None]
    dist_sq = dist_sq + offset_y[:, None, None, :] * offset_y[:, None, None, :]
    phases = WAVENUMBER * jnp.sqrt(dist_sq)
    return (jnp.cos(phases), jnp.sin(phases))

def squared_magnitude(values):
    return values.real * values.real + values.imag * values.imag

def reference(contrast, measured, positions):
    chi = contrast[0] + 1j * contrast[1]
    inc_real, inc_imag = incident(positions, 0, NX)
    incident_field = inc_real + 1j * inc_imag
    data_field = measured[:, 0] + 1j * measured[:, 1]
    green_real, green_imag = green_spectrum(laplace_modes(0, NZ, NZ), laplace_modes(0, NX, NX), laplace_modes(0, NY, NY))
    green = green_real + 1j * green_imag

    def convolve(field, kernel):
        return jnp.fft.ifftn(kernel[None] * jnp.fft.fftn(field, axes=(1, 2, 3)), axes=(1, 2, 3))
    sources_field = chi[None] * incident_field
    scattered = convolve(sources_field, green)
    data_total = jnp.sum(squared_magnitude(data_field))
    for outer_step in range(OUTER):
        object_total = jnp.sum(squared_magnitude(chi[None] * incident_field))
        data_weight = 1.0 / data_total
        object_weight = 1.0 / object_total
        total_field = incident_field + scattered
        residual = chi[None] * total_field - sources_field
        data_residual = data_field - scattered[:, 0]
        adjoint_input = -object_weight * jnp.conj(chi)[None] * residual
        adjoint_input = adjoint_input.at[:, 0].add(data_weight * data_residual)
        descent = object_weight * residual + convolve(adjoint_input, jnp.conj(green))
        descent_image = convolve(descent, green)
        change = descent - chi[None] * descent_image
        step_length = jnp.sum(squared_magnitude(descent)) / (data_weight * jnp.sum(squared_magnitude(descent_image[:, 0])) + object_weight * jnp.sum(squared_magnitude(change)))
        sources_field = sources_field + step_length * descent
        scattered = scattered + step_length * descent_image
        total_field = incident_field + scattered
        numerator = lax.optimization_barrier(jnp.sum(sources_field * jnp.conj(total_field), axis=0))
        power_sum = lax.optimization_barrier(jnp.sum(squared_magnitude(total_field), axis=0))
        floored = jnp.maximum(power_sum, FLOOR_SHARE * SRCS)
        chi_real = jnp.clip(numerator.real / floored, REAL_LOW, REAL_HIGH)
        chi_imag = jnp.clip(numerator.imag / floored, 0.0, IMAG_HIGH)
        chi = chi_real + 1j * chi_imag
    return (jnp.stack([sources_field.real, sources_field.imag], axis=1), jnp.stack([chi.real, chi.imag], axis=0))
```

```python
from functools import partial
import math

import jax
import jax.numpy as jnp
import ml_dtypes
import numpy as np
from jax import lax
from jax.experimental import pallas as pl
from jax.experimental.pallas import tpu as pltpu
from jax.sharding import Mesh, PartitionSpec as P

OUTER = 2
WAVENUMBER = 2.0 * math.pi / 6.0
DAMPING = 0.3
SOURCE_GAP = 8.0
FLOOR_SHARE = 0.75
REAL_LOW = -0.25
REAL_HIGH = 0.35
IMAG_HIGH = 0.1
ALL = ("src", "half", "rest")
GROUP = ("src", "rest")
F32 = jnp.float32


def times_const(value, factor):
    re, im = value
    a, b = factor.real, factor.imag
    if abs(b) < 1e-12:
        return (re, im) if abs(a - 1) < 1e-12 else (re * a, im * a)
    if abs(a) < 1e-12:
        return (im * -b, re * b) if abs(abs(b) - 1) > 1e-12 else ((-im, re) if b > 0 else (im, -re))
    if abs(abs(a) - abs(b)) < 1e-12:
        if a * b > 0:
            return ((re - im) * a, (re + im) * a)
        return ((re + im) * a, (im - re) * a)
    return (re * a - im * b, re * b + im * a)


def small_dft(values, sign):
    count = len(values)
    if count == 1:
        return values
    even, odd = small_dft(values[0::2], sign), small_dft(values[1::2], sign)
    low, high = [], []
    for k in range(count // 2):
        turned = times_const(odd[k], np.exp(sign * 2j * math.pi * k / count))
        low.append((even[k][0] + turned[0], even[k][1] + turned[1]))
        high.append((even[k][0] - turned[0], even[k][1] - turned[1]))
    return low + high


def factors(total):
    bits = total.bit_length() - 1
    return 1 << (bits // 2), total // (1 << (bits // 2))


def stage_one(values, n0, count, sign, keep):
    width = len(values)
    for k1, value in enumerate(small_dft(values, sign)):
        re, im = times_const(value, np.exp(sign * 2j * math.pi * n0 * k1 / count))
        keep[n0 * width + k1, 0] = re
        keep[n0 * width + k1, 1] = im


def stage_two(k1, width, count, sign, keep):
    values = [(keep[n0 * width + k1, 0], keep[n0 * width + k1, 1]) for n0 in range(count // width)]
    return small_dft(values, sign)


def pair(ref, s, z):
    return ref[s, z, 0, 0], ref[s, z, 1, 0]


def put(ref, s, z, value):
    ref[s, z, 0, 0] = value[0]
    ref[s, z, 1, 0] = value[1]


def cell(ref, z):
    return ref[0, z, 0], ref[1, z, 0]


def start_kernel(chi, inc, source, spec, keep):
    sources, depth = inc.shape[:2]
    width, rest = factors(depth)

    def body(s, _):
        for n0 in range(rest):
            values = []
            for n1 in range(width):
                z = n0 + rest * n1
                cr, ci = cell(chi, z)
                er, ei = pair(inc, s, z)
                w = (cr * er - ci * ei, cr * ei + ci * er)
                put(source, s, z, w)
                values.append(w)
            stage_one(values, n0, depth, -1, keep)
        for k1 in range(width):
            for k0, value in enumerate(stage_two(k1, width, depth, -1, keep)):
                put(spec, s, k1 + width * k0, value)
        return 0

    lax.fori_loop(0, sources, body, 0)


def adjoint_kernel(first, scal, field, chi, inc, source, data, *rest_refs):
    if first:
        scat_out, resid, spec, keep_in, keep = rest_refs
    else:
        resid, spec, keep = rest_refs
    sources, depth = inc.shape[:2]
    width, rest = factors(depth)
    object_weight, data_weight = scal[0, 0], scal[0, 1]

    def body(s, _):
        if first:
            for n0 in range(rest):
                stage_one([pair(field, s, n0 + rest * n1) for n1 in range(width)], n0, depth, 1, keep_in)
        for k1 in range(width):
            scattered = stage_two(k1, width, depth, 1, keep_in) if first else None
            values = []
            for k0 in range(rest):
                z = k1 + width * k0
                if first:
                    sr, si = scattered[k0]
                    put(scat_out, s, z, (sr, si))
                else:
                    sr, si = pair(field, s, z)
                cr, ci = cell(chi, z)
                er, ei = pair(inc, s, z)
                wr, wi = pair(source, s, z)
                ur, ui = er + sr, ei + si
                rr = cr * ur - ci * ui - wr
                ri = cr * ui + ci * ur - wi
                put(resid, s, z, (rr, ri))
                vr = -object_weight * (cr * rr + ci * ri)
                vi = -object_weight * (cr * ri - ci * rr)
                if z == 0:
                    vr = vr + data_weight * (data[s, 0, 0] - sr)
                    vi = vi + data_weight * (data[s, 1, 0] - si)
                values.append((vr, vi))
            stage_one(values, k1, depth, -1, keep)
        for j1 in range(rest):
            for j0, value in enumerate(stage_two(j1, rest, depth, -1, keep)):
                put(spec, s, j1 + rest * j0, value)
        return 0

    lax.fori_loop(0, sources, body, 0)


def descent_kernel(scal, field, resid, descent, spec, sums, keep_in, keep):
    sources, depth = resid.shape[:2]
    width, rest = factors(depth)
    object_weight = scal[0, 0]

    def body(s, total):
        for n0 in range(rest):
            stage_one([pair(field, s, n0 + rest * n1) for n1 in range(width)], n0, depth, 1, keep_in)
        for k1 in range(width):
            values = []
            for k0, (gr, gi) in enumerate(stage_two(k1, width, depth, 1, keep_in)):
                z = k1 + width * k0
                rr, ri = pair(resid, s, z)
                dr, di = gr + object_weight * rr, gi + object_weight * ri
                put(descent, s, z, (dr, di))
                total = total + (dr * dr + di * di)
                values.append((dr, di))
            stage_one(values, k1, depth, -1, keep)
        for j1 in range(rest):
            for j0, value in enumerate(stage_two(j1, rest, depth, -1, keep)):
                put(spec, s, j1 + rest * j0, value)
        return total

    sums[0, 0, 0] = lax.fori_loop(0, sources, body, jnp.zeros(sums.shape[3:], F32))


def image_kernel(field, descent, chi, image, sums, keep_in):
    sources, depth = descent.shape[:2]
    width, rest = factors(depth)

    def body(s, totals):
        change, plane = totals
        for n0 in range(rest):
            stage_one([pair(field, s, n0 + rest * n1) for n1 in range(width)], n0, depth, 1, keep_in)
        for k1 in range(width):
            for k0, (hr, hi) in enumerate(stage_two(k1, width, depth, 1, keep_in)):
                z = k1 + width * k0
                put(image, s, z, (hr, hi))
                dr, di = pair(descent, s, z)
                cr, ci = cell(chi, z)
                qr = dr - (cr * hr - ci * hi)
                qi = di - (cr * hi + ci * hr)
                change = change + (qr * qr + qi * qi)
                if z == 0:
                    plane = plane + (hr * hr + hi * hi)
        return change, plane

    zero = jnp.zeros(sums.shape[3:], F32)
    change, plane = lax.fori_loop(0, sources, body, (zero, zero))
    sums[0, 0, 0] = change
    sums[0, 0, 1] = plane


def step_kernel(last, scal, source, descent, scattered, image, inc, source_out, *rest_refs):
    if last:
        (parts,) = rest_refs
    else:
        scat_out, parts = rest_refs
    sources, depth = inc.shape[:2]
    step = scal[0, 0]

    def body(z, _):
        nr = ni = power = None
        for s in range(sources):
            wr, wi = pair(source, s, z)
            dr, di = pair(descent, s, z)
            wr, wi = wr + step * dr, wi + step * di
            put(source_out, s, z, (wr, wi))
            sr, si = pair(scattered, s, z)
            hr, hi = pair(image, s, z)
            sr, si = sr + step * hr, si + step * hi
            if not last:
                put(scat_out, s, z, (sr, si))
            er, ei = pair(inc, s, z)
            ur, ui = er + sr, ei + si
            a, b, c = wr * ur + wi * ui, wi * ur - wr * ui, ur * ur + ui * ui
            nr, ni, power = (a, b, c) if s == 0 else (nr + a, ni + b, power + c)
        parts[0, 0, z] = nr
        parts[0, 1, z] = ni
        parts[0, 2, z] = power
        return 0

    lax.fori_loop(0, depth, body, 0, unroll=4)


def half_tables(total, order):
    half = total // 2
    modes = np.arange(half)[:, None]
    place = np.asarray(order)[None, :]
    out = []
    for odd in (0, 1):
        angle = 2.0 * math.pi * ((2 * modes + odd) * place % total) / total
        cosine, sine = np.cos(angle), np.sin(angle)
        out.append(np.block([[cosine, sine], [-sine, cosine]]).astype(np.float32))
    return np.stack(out)


def high_low(table):
    high = table.astype(ml_dtypes.bfloat16)
    low = (table - high.astype(np.float32)).astype(ml_dtypes.bfloat16)
    return np.stack([high, low])


def lateral_modes(total):
    index = np.concatenate([np.arange(0, total, 2), np.arange(1, total, 2)])
    return (4.0 * np.sin(math.pi * index / total) ** 2).astype(np.float32)


def split(value):
    high = value.astype(jnp.bfloat16)
    return high, (value - high.astype(F32)).astype(jnp.bfloat16)


def left_mul(table, odd, value):
    high, low = split(value)
    return jnp.dot(
        jnp.concatenate([table[0, odd], table[0, odd], table[1, odd]], axis=1),
        jnp.concatenate([high, low, high], axis=0),
        preferred_element_type=F32,
    )


def right_mul(value, table, odd):
    high, low = split(value)
    return jnp.dot(
        jnp.concatenate([high, low, high], axis=1),
        jnp.concatenate([table[0, odd], table[0, odd], table[1, odd]], axis=0),
        preferred_element_type=F32,
    )


def plane_kernel(sign, scale, lz, lx, ly, xf, xb, yf, yb, planes, out):
    senders, _, _, _, rows, ny = planes.shape
    hx, hy = senders * rows, ny // 2
    own = [planes[:, 0, c, 0].reshape(hx, ny) for c in (0, 1)]
    other = [planes[:, 0, c, 1].reshape(hx, ny) for c in (0, 1)]
    across = [
        left_mul(xf, 0, jnp.concatenate([own[0] + other[0], own[1] + other[1]], axis=0)),
        left_mul(xf, 1, jnp.concatenate([own[0] - other[0], own[1] - other[1]], axis=0)),
    ]
    real = jnp.concatenate([across[0][:hx], across[1][:hx]], axis=0)
    imag = jnp.concatenate([across[0][hx:], across[1][hx:]], axis=0)
    wave_sq = WAVENUMBER * WAVENUMBER
    back = []
    for odd in (0, 1):
        flip = -1.0 if odd else 1.0
        folded = jnp.concatenate(
            [real[:, :hy] + flip * real[:, hy:], imag[:, :hy] + flip * imag[:, hy:]], axis=1
        )
        freq = right_mul(folded, yf, odd)
        eigen = (lx[...] + lz[pl.program_id(0)]) + ly[odd]
        real_den = eigen - wave_sq
        imag_den = wave_sq * DAMPING
        factor = (wave_sq * scale) / (real_den * real_den + imag_den * imag_den)
        gr, gi = factor * real_den, factor * (imag_den * sign)
        fr, fi = freq[:, :hy], freq[:, hy:]
        filtered = jnp.concatenate([fr * gr - fi * gi, fr * gi + fi * gr], axis=1)
        back.append(right_mul(filtered, yb, odd))
    plus, minus = back[0] + back[1], back[0] - back[1]
    real = jnp.concatenate([plus[:, :hy], minus[:, :hy]], axis=1)
    imag = jnp.concatenate([plus[:, hy:], minus[:, hy:]], axis=1)
    even = left_mul(xb, 0, jnp.concatenate([real[:hx], imag[:hx]], axis=0))
    odd = left_mul(xb, 1, jnp.concatenate([real[hx:], imag[hx:]], axis=0))
    plus, minus = even + odd, even - odd
    for c in (0, 1):
        out[:, 0, c, 0] = plus[c * hx : (c + 1) * hx].reshape(senders, rows, ny)
        out[:, 0, c, 1] = minus[c * hx : (c + 1) * hx].reshape(senders, rows, ny)


SMEM = pl.BlockSpec(memory_space=pltpu.SMEM)


class Slabs:
    def __init__(self, sources, depth, rows, ny):
        self.sources, self.depth, self.rows, self.ny = sources, depth, rows, ny
        self.lanes = 128 if ny % 128 == 0 else ny
        self.grid = (2, ny // self.lanes)

    def kind(self, name):
        s, z, q, y, lanes = self.sources, self.depth, self.rows, self.ny, self.lanes
        return {
            "field": ((s, z, 2, 2, q, y), (s, z, 2, 1, q, lanes), lambda i, j: (0, 0, 0, i, 0, j)),
            "chi": ((2, z, 2, q, y), (2, z, 1, q, lanes), lambda i, j: (0, 0, i, 0, j)),
            "data": ((s, 2, 2, q, y), (s, 2, 1, q, lanes), lambda i, j: (0, 0, i, 0, j)),
            "parts": ((2, 3, z, q, y), (1, 3, z, q, lanes), lambda i, j: (i, 0, 0, 0, j)),
            "sum1": (self.grid + (1, q, lanes), (1, 1, 1, q, lanes), lambda i, j: (i, j, 0, 0, 0)),
            "sum2": (self.grid + (2, q, lanes), (1, 1, 2, q, lanes), lambda i, j: (i, j, 0, 0, 0)),
        }[name]

    def call(self, kernel, name, ins, outs, scratch, *args):
        def spec(kind):
            if kind == "scal":
                return SMEM
            _, block, index = self.kind(kind)
            return pl.BlockSpec(block, index)

        moved = sum(math.prod(self.kind(k)[0]) * 4 for k in (*ins, *outs) if k != "scal")
        return pl.pallas_call(
            kernel,
            grid=self.grid,
            in_specs=[spec(k) for k in ins],
            out_specs=[spec(k) for k in outs],
            out_shape=[jax.ShapeDtypeStruct(self.kind(k)[0], F32) for k in outs],
            scratch_shapes=[pltpu.VMEM((self.depth, 2, self.rows, self.lanes), F32)] * scratch,
            cost_estimate=pl.CostEstimate(flops=moved * 4, bytes_accessed=moved, transcendentals=0),
            name=name,
        )(*args)


def filter_planes(spectrum, senders, lz, shared, sign, scale):
    _, parts, chunks, rows, ny = spectrum.shape
    planes = spectrum.shape[0] // senders
    shape = (senders, planes, parts, chunks, rows, ny)
    spectrum = spectrum.reshape(shape)
    dense = rows % 8 != 0
    if dense:
        spectrum = spectrum.transpose(1, 2, 3, 0, 4, 5).reshape(1, planes, parts, chunks, senders * rows, ny)
    block = (spectrum.shape[0], 1) + spectrum.shape[2:]
    at = lambda i: (0, i, 0, 0, 0, 0)
    whole = lambda t: pl.BlockSpec(t.shape, lambda i, n=t.ndim: (0,) * n)
    nx = 2 * senders * rows
    out = pl.pallas_call(
        partial(plane_kernel, sign, scale),
        grid=(planes,),
        in_specs=[SMEM] + [whole(t) for t in shared] + [pl.BlockSpec(block, at)],
        out_specs=pl.BlockSpec(block, at),
        out_shape=jax.ShapeDtypeStruct(spectrum.shape, F32),
        cost_estimate=pl.CostEstimate(
            flops=planes * 24 * nx * nx * ny * 2, bytes_accessed=2 * spectrum.size * 4, transcendentals=0
        ),
        name="planes",
    )(lz, *shared, spectrum)
    if dense:
        out = out.reshape(planes, parts, chunks, senders, rows, ny).transpose(3, 0, 1, 2, 4, 5)
    return out.reshape(senders * planes, parts, chunks, rows, ny)


def everyone(values):
    count = math.prod(lax.axis_size(name) for name in ALL)
    row = jnp.zeros((128,), F32).at[: len(values)].set(jnp.stack(values))
    sent = jnp.broadcast_to(row[None], (count, 128))
    return jnp.sum(lax.all_to_all(sent, ALL, 0, 0, tiled=True), axis=0)


def swap_halves(value):
    return lax.ppermute(value, "half", [(0, 1), (1, 0)])


def bounded(numer_real, numer_imag, power, total_sources):
    floored = jnp.maximum(power, FLOOR_SHARE * total_sources)
    return jnp.stack(
        [
            jnp.clip(numer_real / floored, REAL_LOW, REAL_HIGH),
            jnp.clip(numer_imag / floored, 0.0, IMAG_HIGH),
        ]
    )


def on_device(contrast, measured, positions):
    shares, rest_count = lax.axis_size("src"), lax.axis_size("rest")
    share, half, rest = (lax.axis_index(name) for name in ALL)
    senders = shares * rest_count
    _, depth, block_rows, ny = contrast.shape
    rows = block_rows // shares
    nx = block_rows * 2 * rest_count
    per_share = positions.shape[0]
    total_sources = per_share * shares
    sources = total_sources // 2
    slabs = Slabs(sources, depth, rows, ny)

    chi_own = lax.dynamic_index_in_dim(
        contrast.reshape(2, depth, shares, rows, ny), share, axis=2, keepdims=False
    )
    chi_other = swap_halves(chi_own)

    sent = jnp.concatenate(
        [
            measured.reshape(per_share, 2, shares, rows * ny).transpose(2, 0, 1, 3).reshape(shares, -1),
            jnp.broadcast_to(jnp.pad(positions.astype(F32).reshape(1, -1), ((0, 0), (0, 126))), (shares, 2 * per_share + 126)),
        ],
        axis=1,
    )
    got = lax.all_to_all(sent, "src", 0, 0, tiled=True)
    cells = per_share * 2 * rows * ny
    data_own = got[:, :cells].reshape(total_sources, 2, rows, ny)
    spots = got[:, cells : cells + 2 * per_share].reshape(total_sources, 2)
    mine = lambda v, h: lax.dynamic_slice_in_dim(v, h * sources, sources, axis=0)
    data = jnp.stack([mine(data_own, half), swap_halves(mine(data_own, 1 - half))], axis=2)
    spots = mine(spots, half)

    heights = jnp.arange(depth).astype(F32) + SOURCE_GAP
    starts = (jnp.stack([half, 1 - half]) * rest_count + rest) * block_rows + share * rows
    across = (starts[:, None] + jnp.arange(rows)[None, :]).astype(F32)
    offset_x = across[None] - spots[:, 0][:, None, None]
    offset_y = jnp.arange(ny).astype(F32)[None] - spots[:, 1][:, None]
    dist_sq = (heights * heights)[None, :, None, None, None] + (offset_x * offset_x)[:, None, :, :, None]
    dist_sq = dist_sq + (offset_y * offset_y)[:, None, None, None, :]
    phases = WAVENUMBER * jnp.sqrt(dist_sq)
    inc = jnp.stack([jnp.cos(phases), jnp.sin(phases)], axis=2)

    order = [(k * shares + a) * rows + q for a in range(shares) for k in range(rest_count) for q in range(rows)]
    x_table, y_table = half_tables(nx, order), half_tables(ny, range(ny // 2))
    flip = lambda t: high_low(np.swapaxes(t, -1, -2))
    lx = np.broadcast_to(lateral_modes(nx)[:, None], (nx, ny // 2))
    ly = lateral_modes(ny).reshape(2, 1, ny // 2)
    shared = [jnp.asarray(t) for t in (lx, ly, high_low(x_table), flip(x_table), flip(y_table), high_low(y_table))]
    planes = sources * depth // senders
    place = share * rest_count + rest
    modes = (place * planes + jnp.arange(planes)) % depth
    half_sine = jnp.sin(math.pi * modes.astype(F32) / depth)
    lz = 4.0 * half_sine * half_sine
    scale = 1.0 / (nx * ny * depth)

    def convolve(spec, sign):
        flat = spec.reshape(sources * depth, 2, 2, rows, ny)
        flat = lax.all_to_all(flat, GROUP, 0, 0, tiled=True)
        flat = filter_planes(flat, senders, lz, shared, sign, scale)
        return lax.all_to_all(flat, GROUP, 0, 0, tiled=True).reshape(spec.shape)

    totals = everyone([jnp.sum(measured * measured), total_sources * jnp.sum(chi_own * chi_own)])
    data_weight = 1.0 / totals[0]
    object_total = totals[1]
    chi = jnp.stack([chi_own, chi_other], axis=2)
    source, spec = slabs.call(start_kernel, "start", ("chi", "field"), ("field", "field"), 1, chi, inc)
    scattered = convolve(spec, 1.0)
    for outer in range(OUTER):
        object_weight = 1.0 / object_total
        weights = jnp.stack([object_weight, data_weight]).reshape(1, 2)
        first, last = outer == 0, outer == OUTER - 1
        out = slabs.call(
            partial(adjoint_kernel, first),
            "adjoint",
            ("scal", "field", "chi", "field", "field", "data"),
            ("field",) * (3 if first else 2),
            2 if first else 1,
            weights, scattered, chi, inc, source, data,
        )
        if first:
            scattered, resid, spec = out
        else:
            resid, spec = out
        descent, spec, sum_d = slabs.call(
            descent_kernel, "descent", ("scal", "field", "field"), ("field", "field", "sum1"), 2,
            weights, convolve(spec, -1.0), resid,
        )
        image, sum_q = slabs.call(
            image_kernel, "image", ("field", "field", "chi"), ("field", "sum2"), 1,
            convolve(spec, 1.0), descent, chi,
        )
        totals = everyone([jnp.sum(sum_d), jnp.sum(sum_q[:, :, 0]), jnp.sum(sum_q[:, :, 1])])
        step = totals[0] / (data_weight * totals[2] + object_weight * totals[1])
        out = slabs.call(
            partial(step_kernel, last),
            "step",
            ("scal",) + ("field",) * 5,
            ("field",) * (1 if last else 2) + ("parts",),
            0,
            step.reshape(1, 1), source, descent, scattered, image, inc,
        )
        if last:
            source, parts = out
        else:
            source, scattered, parts = out
        sums = parts[0] + swap_halves(parts[1])
        chi_own = bounded(sums[0], sums[1], sums[2], total_sources)
        if not last:
            chi = jnp.stack([chi_own, swap_halves(chi_own)], axis=2)
            object_total = everyone([total_sources * jnp.sum(chi_own * chi_own)])[0]

    own, theirs = source[:, :, :, 0], swap_halves(source[:, :, :, 1])
    lower, upper = jnp.where(half == 0, own, theirs), jnp.where(half == 0, theirs, own)
    fields = jnp.concatenate([lower, upper], axis=0)
    fields = lax.all_to_all(fields, "src", 0, 0, tiled=True)
    fields = fields.reshape(shares, per_share, depth, 2, rows, ny).transpose(1, 3, 2, 0, 4, 5)
    fields = fields.reshape(per_share, 2, depth, block_rows, ny)
    sent = jnp.broadcast_to(chi_own[None], (shares,) + chi_own.shape)
    contrast_new = lax.all_to_all(sent, "src", 0, 0, tiled=True)
    contrast_new = contrast_new.transpose(1, 2, 0, 3, 4).reshape(contrast.shape)
    return fields, contrast_new


def solution(mesh):
    shares, spaces = mesh.shape["src"], mesh.shape["space"]
    split_mesh = Mesh(mesh.devices.reshape(shares, 2, spaces // 2), ALL)
    space = ("half", "rest")
    return jax.shard_map(
        on_device,
        mesh=split_mesh,
        in_specs=(P(None, None, space, None), P("src", None, space, None), P("src", None)),
        out_specs=(P("src", None, None, space, None), P(None, None, space, None)),
        check_vma=False,
    )
```

```python
from functools import partial
import math

import jax
import jax.numpy as jnp
import ml_dtypes
import numpy as np
from jax import lax
from jax.experimental import pallas as pl
from jax.experimental.pallas import tpu as pltpu
from jax.sharding import Mesh, PartitionSpec as P

OUTER = 2
WAVENUMBER = 2.0 * math.pi / 6.0
DAMPING = 0.3
SOURCE_GAP = 8.0
FLOOR_SHARE = 0.75
REAL_LOW = -0.25
REAL_HIGH = 0.35
IMAG_HIGH = 0.1
ALL = ("src", "half", "rest")
GROUP = ("src", "rest")
F32 = jnp.float32


def times_const(value, factor):
    re, im = value
    a, b = factor.real, factor.imag
    if abs(b) < 1e-12:
        return (re, im) if abs(a - 1) < 1e-12 else (re * a, im * a)
    if abs(a) < 1e-12:
        return (im * -b, re * b) if abs(abs(b) - 1) > 1e-12 else ((-im, re) if b > 0 else (im, -re))
    if abs(abs(a) - abs(b)) < 1e-12:
        if a * b > 0:
            return ((re - im) * a, (re + im) * a)
        return ((re + im) * a, (im - re) * a)
    return (re * a - im * b, re * b + im * a)


def small_dft(values, sign):
    count = len(values)
    if count == 1:
        return values
    even, odd = small_dft(values[0::2], sign), small_dft(values[1::2], sign)
    low, high = [], []
    for k in range(count // 2):
        turned = times_const(odd[k], np.exp(sign * 2j * math.pi * k / count))
        low.append((even[k][0] + turned[0], even[k][1] + turned[1]))
        high.append((even[k][0] - turned[0], even[k][1] - turned[1]))
    return low + high


def factors(total):
    bits = total.bit_length() - 1
    return 1 << (bits // 2), total // (1 << (bits // 2))


def stage_one(values, n0, count, sign, keep):
    width = len(values)
    for k1, value in enumerate(small_dft(values, sign)):
        re, im = times_const(value, np.exp(sign * 2j * math.pi * n0 * k1 / count))
        keep[n0 * width + k1, 0] = re
        keep[n0 * width + k1, 1] = im


def stage_two(k1, width, count, sign, keep):
    values = [(keep[n0 * width + k1, 0], keep[n0 * width + k1, 1]) for n0 in range(count // width)]
    return small_dft(values, sign)


def pair(ref, z):
    return ref[0, z, 0], ref[0, z, 1]


def put(ref, z, value):
    ref[0, z, 0] = value[0]
    ref[0, z, 1] = value[1]


def put_spec(ref, z, value):
    ref[z, 0] = value[0]
    ref[z, 1] = value[1]


def returned(refs, z):
    place, plane = divmod(z, sum(ref.shape[1] for ref in refs))
    for ref in refs:
        if plane < ref.shape[1]:
            return ref[place, plane, 0, 0], ref[place, plane, 1, 0]
        plane -= ref.shape[1]


def invert_one(refs, depth, width, rest, keep):
    for n0 in range(rest):
        stage_one([returned(refs, n0 + rest * n1) for n1 in range(width)], n0, depth, 1, keep)


def finish(spec, depth, width, rest, keep):
    for j1 in range(rest):
        for j0, value in enumerate(stage_two(j1, rest, depth, -1, keep)):
            put_spec(spec, j1 + rest * j0, value)


def start_kernel(chi, inc, source, spec, keep):
    depth = inc.shape[1]
    width, rest = factors(depth)
    for n0 in range(width):
        values = []
        for n1 in range(rest):
            z = n0 + width * n1
            cr, ci = chi[0, z], chi[1, z]
            er, ei = pair(inc, z)
            w = (cr * er - ci * ei, cr * ei + ci * er)
            put(source, z, w)
            values.append(w)
        stage_one(values, n0, depth, -1, keep)
    finish(spec, depth, width, rest, keep)


def adjoint_kernel(first, scal, chi, inc, source, data, *refs):
    if first:
        *fields, scat_out, resid, spec, keep_in, keep = refs
    else:
        field, resid, spec, keep = refs
    depth = inc.shape[1]
    width, rest = factors(depth)
    object_weight, data_weight = scal[0, 0], scal[0, 1]
    if first:
        invert_one(fields, depth, width, rest, keep_in)
    for k1 in range(width):
        scattered = stage_two(k1, width, depth, 1, keep_in) if first else None
        values = []
        for k0 in range(rest):
            z = k1 + width * k0
            if first:
                sr, si = scattered[k0]
                put(scat_out, z, (sr, si))
            else:
                sr, si = pair(field, z)
            cr, ci = chi[0, z], chi[1, z]
            er, ei = pair(inc, z)
            wr, wi = pair(source, z)
            ur, ui = er + sr, ei + si
            rr = cr * ur - ci * ui - wr
            ri = cr * ui + ci * ur - wi
            put(resid, z, (rr, ri))
            vr = -object_weight * (cr * rr + ci * ri)
            vi = -object_weight * (cr * ri - ci * rr)
            if z == 0:
                vr = vr + data_weight * (data[0, 0] - sr)
                vi = vi + data_weight * (data[0, 1] - si)
            values.append((vr, vi))
        stage_one(values, k1, depth, -1, keep)
    finish(spec, depth, width, rest, keep)


def descent_kernel(scal, resid, *refs):
    *fields, descent, spec, sums, keep_in, keep = refs
    depth = resid.shape[1]
    width, rest = factors(depth)
    object_weight = scal[0, 0]
    invert_one(fields, depth, width, rest, keep_in)
    total = jnp.zeros(sums.shape[3:], F32)
    for k1 in range(width):
        values = []
        for k0, (gr, gi) in enumerate(stage_two(k1, width, depth, 1, keep_in)):
            z = k1 + width * k0
            rr, ri = pair(resid, z)
            dr, di = gr + object_weight * rr, gi + object_weight * ri
            put(descent, z, (dr, di))
            total = total + (dr * dr + di * di)
            values.append((dr, di))
        stage_one(values, k1, depth, -1, keep)
    finish(spec, depth, width, rest, keep)
    sums[0, 0, 0] = total


def image_kernel(descent, chi, *refs):
    *fields, image, sums, keep_in = refs
    depth = descent.shape[1]
    width, rest = factors(depth)
    invert_one(fields, depth, width, rest, keep_in)
    change = plane = jnp.zeros(sums.shape[3:], F32)
    for k1 in range(width):
        for k0, (hr, hi) in enumerate(stage_two(k1, width, depth, 1, keep_in)):
            z = k1 + width * k0
            put(image, z, (hr, hi))
            dr, di = pair(descent, z)
            cr, ci = chi[0, z], chi[1, z]
            qr = dr - (cr * hr - ci * hi)
            qi = di - (cr * hi + ci * hr)
            change = change + (qr * qr + qi * qi)
            if z == 0:
                plane = hr * hr + hi * hi
    sums[0, 0, 0] = change
    sums[0, 0, 1] = plane


def step_kernel(last, scal, source, descent, scattered, image, inc, source_out, *rest_refs):
    if last:
        (parts,) = rest_refs
    else:
        scat_out, parts = rest_refs
    sources, depth = inc.shape[:2]
    step = scal[0, 0]

    def body(z, _):
        nr = ni = power = None
        for s in range(sources):
            dr, di = descent[s, z, 0], descent[s, z, 1]
            wr, wi = source[s, z, 0] + step * dr, source[s, z, 1] + step * di
            source_out[s, z, 0] = wr
            source_out[s, z, 1] = wi
            sr = scattered[s, z, 0] + step * image[s, z, 0]
            si = scattered[s, z, 1] + step * image[s, z, 1]
            if not last:
                scat_out[s, z, 0] = sr
                scat_out[s, z, 1] = si
            ur, ui = inc[s, z, 0] + sr, inc[s, z, 1] + si
            a, b, c = wr * ur + wi * ui, wi * ur - wr * ui, ur * ur + ui * ui
            nr, ni, power = (a, b, c) if s == 0 else (nr + a, ni + b, power + c)
        parts[0, z] = nr
        parts[1, z] = ni
        parts[2, z] = power
        return 0

    lax.fori_loop(0, depth, body, 0, unroll=4)


def assemble_kernel(spot, *refs):
    *rounds, out = refs
    turn = lax.rem(spot[0] + len(rounds) - pl.program_id(0), len(rounds))
    for t, ref in enumerate(rounds):

        @pl.when(turn == t)
        def _(ref=ref):
            for z in range(out.shape[2]):
                out[:, 0, z] = ref[:, z, 0]
                out[:, 1, z] = ref[:, z, 1]


def half_tables(total, order):
    half = total // 2
    modes = np.arange(half)[:, None]
    place = np.asarray(order)[None, :]
    out = []
    for odd in (0, 1):
        angle = 2.0 * math.pi * ((2 * modes + odd) * place % total) / total
        cosine, sine = np.cos(angle), np.sin(angle)
        out.append(np.block([[cosine, sine], [-sine, cosine]]).astype(np.float32))
    return np.stack(out)


def high_low(table):
    high = table.astype(ml_dtypes.bfloat16)
    low = (table - high.astype(np.float32)).astype(ml_dtypes.bfloat16)
    return np.stack([high, low])


def lateral_modes(total):
    index = np.concatenate([np.arange(0, total, 2), np.arange(1, total, 2)])
    return (4.0 * np.sin(math.pi * index / total) ** 2).astype(np.float32)


def split(value):
    high = value.astype(jnp.bfloat16)
    return high, (value - high.astype(F32)).astype(jnp.bfloat16)


def left_mul(table, odd, value):
    high, low = split(value)
    return jnp.dot(
        jnp.concatenate([table[0, odd], table[0, odd], table[1, odd]], axis=1),
        jnp.concatenate([high, low, high], axis=0),
        preferred_element_type=F32,
    )


def right_mul(value, table, odd):
    high, low = split(value)
    return jnp.dot(
        jnp.concatenate([high, low, high], axis=1),
        jnp.concatenate([table[0, odd], table[0, odd], table[1, odd]], axis=0),
        preferred_element_type=F32,
    )


def plane_kernel(sign, scale, lz, lx, ly, xf, xb, yf, yb, own_ref, other_ref, out):
    senders, _, _, rows, ny = own_ref.shape
    hx, hy = senders * rows, ny // 2
    own = [own_ref[:, 0, c].reshape(hx, ny) for c in (0, 1)]
    other = [other_ref[:, 0, c].reshape(hx, ny) for c in (0, 1)]
    across = [
        left_mul(xf, 0, jnp.concatenate([own[0] + other[0], own[1] + other[1]], axis=0)),
        left_mul(xf, 1, jnp.concatenate([own[0] - other[0], own[1] - other[1]], axis=0)),
    ]
    real = jnp.concatenate([across[0][:hx], across[1][:hx]], axis=0)
    imag = jnp.concatenate([across[0][hx:], across[1][hx:]], axis=0)
    wave_sq = WAVENUMBER * WAVENUMBER
    back = []
    for odd in (0, 1):
        flip = -1.0 if odd else 1.0
        folded = jnp.concatenate(
            [real[:, :hy] + flip * real[:, hy:], imag[:, :hy] + flip * imag[:, hy:]], axis=1
        )
        freq = right_mul(folded, yf, odd)
        eigen = (lx[...] + lz[pl.program_id(0)]) + ly[odd]
        real_den = eigen - wave_sq
        imag_den = wave_sq * DAMPING
        factor = (wave_sq * scale) / (real_den * real_den + imag_den * imag_den)
        gr, gi = factor * real_den, factor * (imag_den * sign)
        fr, fi = freq[:, :hy], freq[:, hy:]
        filtered = jnp.concatenate([fr * gr - fi * gi, fr * gi + fi * gr], axis=1)
        back.append(right_mul(filtered, yb, odd))
    plus, minus = back[0] + back[1], back[0] - back[1]
    real = jnp.concatenate([plus[:, :hy], minus[:, :hy]], axis=1)
    imag = jnp.concatenate([plus[:, hy:], minus[:, hy:]], axis=1)
    even = left_mul(xb, 0, jnp.concatenate([real[:hx], imag[:hx]], axis=0))
    odd = left_mul(xb, 1, jnp.concatenate([real[hx:], imag[hx:]], axis=0))
    plus, minus = even + odd, even - odd
    for c in (0, 1):
        out[:, 0, c, 0] = plus[c * hx : (c + 1) * hx].reshape(senders, rows, ny)
        out[:, 0, c, 1] = minus[c * hx : (c + 1) * hx].reshape(senders, rows, ny)


SMEM = pl.BlockSpec(memory_space=pltpu.SMEM)


class Slabs:
    def __init__(self, sources, depth, rows, ny, pieces):
        self.sources, self.depth, self.rows, self.ny, self.pieces = sources, depth, rows, ny, pieces
        self.lanes = 128 if ny % 128 == 0 else ny
        self.deep = depth // 4 if depth % 4 == 0 else depth

    def kind(self, name, chunk):
        s, z, q, y, lanes, deep = self.sources, self.depth, self.rows, self.ny, self.lanes, self.deep
        turns = (y // lanes, s)
        if name.startswith("piece"):
            count = self.pieces[int(name[5:])]
            owners = z // sum(self.pieces)
            return (
                (s * owners, count, 2, 2, q, y),
                (owners, count, 2, 1, q, lanes),
                lambda j, i: (i, 0, 0, chunk, 0, j),
            )
        return {
            "field": ((s, z, 2, q, y), (1, z, 2, q, lanes), lambda j, i: (i, 0, 0, 0, j)),
            "spec": ((s * z, 2, q, y), (z, 2, q, lanes), lambda j, i: (i, 0, 0, j)),
            "chi": ((2, z, q, y), (2, z, q, lanes), lambda j, i: (0, 0, 0, j)),
            "data": ((s, 2, q, y), (1, 2, q, lanes), lambda j, i: (i, 0, 0, j)),
            "sum1": (turns + (1, q, lanes), (1, 1, 1, q, lanes), lambda j, i: (j, i, 0, 0, 0)),
            "sum2": (turns + (2, q, lanes), (1, 1, 2, q, lanes), lambda j, i: (j, i, 0, 0, 0)),
            "every": ((s, z, 2, q, y), (s, deep, 2, q, lanes), lambda j, i: (0, i, 0, 0, j)),
            "parts": ((3, z, q, y), (3, deep, q, lanes), lambda j, i: (0, i, 0, j)),
        }[name]

    def call(self, kernel, name, chunk, ins, outs, scratch, *args):
        def spec(kind):
            if kind == "scal":
                return SMEM
            _, block, index = self.kind(kind, chunk)
            return pl.BlockSpec(block, index)

        sizes = [math.prod(self.kind(k, chunk)[0]) * 4 for k in (*ins, *outs) if k != "scal"]
        moved = sum(sizes)
        second = self.depth // self.deep if "parts" in outs else self.sources
        return pl.pallas_call(
            kernel,
            grid=(self.ny // self.lanes, second),
            in_specs=[spec(k) for k in ins],
            out_specs=[spec(k) for k in outs],
            out_shape=[jax.ShapeDtypeStruct(self.kind(k, chunk)[0], F32) for k in outs],
            scratch_shapes=[pltpu.VMEM((self.depth, 2, self.rows, self.lanes), F32)] * scratch,
            cost_estimate=pl.CostEstimate(flops=moved * 4, bytes_accessed=moved, transcendentals=0),
            name=name,
        )(*args)

    def piece_kinds(self):
        return tuple("piece%d" % m for m in range(len(self.pieces)))


def filter_planes(own, other, first, count, senders, lz, shared, sign, scale):
    _, parts, rows, ny = own.shape
    planes = own.shape[0] // senders
    dense = rows % 8 != 0

    def shaped(value):
        value = value.reshape(senders, planes, parts, rows, ny)
        if dense:
            value = value.transpose(1, 2, 0, 3, 4).reshape(1, planes, parts, senders * rows, ny)
        return value

    own, other = shaped(own), shaped(other)
    lead, deep = own.shape[0], own.shape[3]
    out_shape = (lead, count, parts, 2, deep, ny)
    whole = lambda t: pl.BlockSpec(t.shape, lambda i, n=t.ndim: (0,) * n)
    block = pl.BlockSpec((lead, 1, parts, deep, ny), lambda i: (0, i + first, 0, 0, 0))
    nx = 2 * senders * rows
    out = pl.pallas_call(
        partial(plane_kernel, sign, scale),
        grid=(count,),
        in_specs=[SMEM] + [whole(t) for t in shared] + [block, block],
        out_specs=pl.BlockSpec((lead, 1, parts, 2, deep, ny), lambda i: (0, i, 0, 0, 0, 0)),
        out_shape=jax.ShapeDtypeStruct(out_shape, F32),
        cost_estimate=pl.CostEstimate(
            flops=count * 24 * nx * nx * ny * 2,
            bytes_accessed=2 * math.prod(out_shape) * 4,
            transcendentals=0,
        ),
        name="planes",
    )(lz[first : first + count], *shared, own, other)
    if dense:
        out = out.reshape(count, parts, 2, senders, rows, ny).transpose(3, 0, 1, 2, 4, 5)
    return out


def everyone(values):
    count = math.prod(lax.axis_size(name) for name in ALL)
    row = jnp.zeros((128,), F32).at[: len(values)].set(jnp.stack(values))
    sent = jnp.broadcast_to(row[None], (count, 128))
    return jnp.sum(lax.all_to_all(sent, ALL, 0, 0, tiled=True), axis=0)


def swap_halves(value):
    return lax.ppermute(value, "half", [(0, 1), (1, 0)])


def after(value, *others):
    return lax.optimization_barrier((value, *others))[0]


def bounded(numer_real, numer_imag, power, total_sources):
    floored = jnp.maximum(power, FLOOR_SHARE * total_sources)
    return jnp.stack(
        [
            jnp.clip(numer_real / floored, REAL_LOW, REAL_HIGH),
            jnp.clip(numer_imag / floored, 0.0, IMAG_HIGH),
        ]
    )


def deliver(chunks, shares, per_share, share, half, gate):
    slots = shares // 2
    rounds = []
    for t in range(shares):
        number = lax.rem(share + t, shares)
        slot = number // 2
        cut = [lax.dynamic_slice_in_dim(w, slot * per_share, per_share, axis=0) for w in chunks]
        sent = after(jnp.where(number % 2 == 0, cut[0], cut[1]), gate)
        pairs = []
        for a in range(shares):
            g, c = divmod((a + t) % shares, 2)
            for h in (0, 1):
                pairs.append((a * 2 + h, (h * slots + g) * 2 + (h + c) % 2))
        rounds.append(lax.ppermute(sent, ("src", "half"), pairs))
    spot = 2 * lax.rem(share, slots) + lax.rem(half + share // slots, 2)
    _, depth, _, rows, ny = rounds[0].shape
    whole = pl.BlockSpec(rounds[0].shape, lambda a: (0, 0, 0, 0, 0))
    out = pl.pallas_call(
        assemble_kernel,
        grid=(shares,),
        in_specs=[SMEM] + [whole] * shares,
        out_specs=pl.BlockSpec((per_share, 2, depth, None, rows, ny), lambda a: (0, 0, 0, a, 0, 0)),
        out_shape=jax.ShapeDtypeStruct((per_share, 2, depth, shares, rows, ny), F32),
        name="assemble",
    )(spot.reshape(1).astype(jnp.int32), *rounds)
    return out.reshape(per_share, 2, depth, shares * rows, ny)


def on_device(contrast, measured, positions):
    shares, rest_count = lax.axis_size("src"), lax.axis_size("rest")
    share, half, rest = (lax.axis_index(name) for name in ALL)
    senders = shares * rest_count
    _, depth, block_rows, ny = contrast.shape
    rows = block_rows // shares
    nx = block_rows * 2 * rest_count
    per_share = positions.shape[0]
    total_sources = per_share * shares
    sources = total_sources // 2
    planes = sources * depth // senders
    pieces = (planes // 4, planes - planes // 4) if planes >= 4 else (planes,)
    slabs = Slabs(sources, depth, rows, ny, pieces)

    chi_own = lax.dynamic_index_in_dim(
        contrast.reshape(2, depth, shares, rows, ny), share, axis=2, keepdims=False
    )
    chi = [chi_own, swap_halves(chi_own)]

    spots = jnp.pad(positions.astype(F32).reshape(1, -1), ((0, 0), (0, 126)))
    sent = jnp.concatenate(
        [
            measured.reshape(per_share, 2, shares, rows * ny).transpose(2, 0, 1, 3).reshape(shares, -1),
            jnp.broadcast_to(spots, (shares, spots.shape[1])),
        ],
        axis=1,
    )
    got = lax.all_to_all(sent, "src", 0, 0, tiled=True)
    cells = per_share * 2 * rows * ny
    data_own = got[:, :cells].reshape(total_sources, 2, rows, ny)
    spots = got[:, cells : cells + 2 * per_share].reshape(total_sources, 2)
    mine = lambda v, h: lax.dynamic_slice_in_dim(v, h * sources, sources, axis=0)
    data = [mine(data_own, half), swap_halves(mine(data_own, 1 - half))]
    spots = mine(spots, half)

    heights = jnp.arange(depth).astype(F32) + SOURCE_GAP
    offset_y = jnp.arange(ny).astype(F32)[None] - spots[:, 1][:, None]
    inc = []
    for where in (half, 1 - half):
        start = (where * rest_count + rest) * block_rows + share * rows
        offset_x = (start + jnp.arange(rows)).astype(F32)[None] - spots[:, 0][:, None]
        dist_sq = (heights * heights)[None, :, None, None] + (offset_x * offset_x)[:, None, :, None]
        dist_sq = dist_sq + (offset_y * offset_y)[:, None, None, :]
        phases = WAVENUMBER * jnp.sqrt(dist_sq)
        inc.append(jnp.stack([jnp.cos(phases), jnp.sin(phases)], axis=2))

    order = [(k * shares + a) * rows + q for a in range(shares) for k in range(rest_count) for q in range(rows)]
    x_table, y_table = half_tables(nx, order), half_tables(ny, range(ny // 2))
    flip = lambda t: high_low(np.swapaxes(t, -1, -2))
    lx = np.broadcast_to(lateral_modes(nx)[:, None], (nx, ny // 2))
    ly = lateral_modes(ny).reshape(2, 1, ny // 2)
    shared = [jnp.asarray(t) for t in (lx, ly, high_low(x_table), flip(x_table), flip(y_table), high_low(y_table))]
    place = share * rest_count + rest
    modes = (place * planes + jnp.arange(planes)) % depth
    half_sine = jnp.sin(math.pi * modes.astype(F32) / depth)
    lz = 4.0 * half_sine * half_sine
    scale = 1.0 / (nx * ny * depth)

    def forward(spec):
        return lax.all_to_all(spec, GROUP, 0, 0, tiled=True)

    def back(came, sign):
        out, first = [], 0
        for count in pieces:
            part = filter_planes(*came, first, count, senders, lz, shared, sign, scale)
            shape = part.shape
            part = lax.all_to_all(part.reshape((-1,) + shape[2:]), GROUP, 0, 0, tiled=True)
            out.append(part.reshape(shape))
            first += count
        return out

    both = (0, 1)
    piece_kinds = slabs.piece_kinds()
    totals = everyone([jnp.sum(measured * measured), total_sources * jnp.sum(chi_own * chi_own)])
    data_weight = 1.0 / totals[0]
    object_total = totals[1]
    source, came = [None, None], [None, None]
    for c in both:
        source[c], spec = slabs.call(
            start_kernel, "start", c, ("chi", "field"), ("field", "spec"), 1, chi[c], inc[c]
        )
        came[c] = forward(spec)
    fields = back(came, 1.0)
    scattered = [None, None]
    for outer in range(OUTER):
        object_weight = 1.0 / object_total
        weights = jnp.stack([object_weight, data_weight]).reshape(1, 2)
        first, last = outer == 0, outer == OUTER - 1
        resid, descent, image = [None, None], [None, None], [None, None]
        came = [None, None]
        for c in both:
            out = slabs.call(
                partial(adjoint_kernel, first),
                "adjoint",
                c,
                ("scal", "chi", "field", "field", "data") + (piece_kinds if first else ("field",)),
                ("field", "field", "spec") if first else ("field", "spec"),
                2 if first else 1,
                weights, chi[c], inc[c], source[c], data[c], *(fields if first else (scattered[c],)),
            )
            if first:
                scattered[c] = out[0]
            resid[c] = out[-2]
            came[c] = forward(out[-1])
        fields = back(came, -1.0)
        came, sums = [None, None], []
        for c in both:
            descent[c], spec, part = slabs.call(
                descent_kernel, "descent", c, ("scal", "field") + piece_kinds, ("field", "spec", "sum1"), 2,
                weights, resid[c], *fields,
            )
            came[c] = forward(spec)
            sums.append(part)
        sum_d = jnp.sum(sums[0]) + jnp.sum(sums[1])
        fields = back(came, 1.0)
        sums = []
        for c in both:
            image[c], part = slabs.call(
                image_kernel, "image", c, ("field", "chi") + piece_kinds, ("field", "sum2"), 1,
                descent[c], chi[c], *fields,
            )
            sums.append(part)
        sum_q = sums[0] + sums[1]
        totals = everyone([sum_d, jnp.sum(sum_q[:, :, 0]), jnp.sum(sum_q[:, :, 1])])
        step = totals[0] / (data_weight * totals[2] + object_weight * totals[1])
        parts = [None, None]
        for c in (1, 0):
            out = slabs.call(
                partial(step_kernel, last),
                "step",
                c,
                ("scal",) + ("every",) * 5,
                ("every",) * (1 if last else 2) + ("parts",),
                0,
                step.reshape(1, 1), source[c], descent[c], scattered[c], image[c], inc[c],
            )
            source[c], parts[c] = out[0], out[-1]
            if not last:
                scattered[c] = out[1]
        received = swap_halves(parts[1])
        sums = parts[0] + received
        chi_own = bounded(sums[0], sums[1], sums[2], total_sources)
        if not last:
            object_total = everyone([total_sources * jnp.sum(chi_own * chi_own)])[0]
            chi = [chi_own, swap_halves(after(chi_own, object_total))]

    contrast_sources = deliver(source, shares, per_share, share, half, received)
    sent = jnp.broadcast_to(chi_own[None], (shares,) + chi_own.shape)
    contrast_new = lax.all_to_all(sent, "src", 0, 0, tiled=True)
    contrast_new = contrast_new.transpose(1, 2, 0, 3, 4).reshape(contrast.shape)
    return contrast_sources, contrast_new


def solution(mesh):
    shares, spaces = mesh.shape["src"], mesh.shape["space"]
    split_mesh = Mesh(mesh.devices.reshape(shares, 2, spaces // 2), ALL)
    space = ("half", "rest")
    return jax.shard_map(
        on_device,
        mesh=split_mesh,
        in_specs=(P(None, None, space, None), P("src", None, space, None), P("src", None)),
        out_specs=(P("src", None, None, space, None), P(None, None, space, None)),
        check_vma=False,
    )
```

```python
from functools import partial
import math

import jax
import jax.numpy as jnp
import ml_dtypes
import numpy as np
from jax import lax
from jax.experimental import pallas as pl
from jax.experimental.pallas import tpu as pltpu
from jax.sharding import Mesh, PartitionSpec as P


OUTER = 2
WAVENUMBER = 2.0 * math.pi / 6.0
DAMPING = 0.3
SOURCE_GAP = 8.0
FLOOR_SHARE = 0.75
REAL_LOW = -0.25
REAL_HIGH = 0.35
IMAG_HIGH = 0.1
ALL = ("src", "half", "rest")
GROUP = ("src", "rest")
F32 = jnp.float32


def times_const(value, factor):
    re, im = value
    a, b = factor.real, factor.imag
    if abs(b) < 1e-12:
        return (re, im) if abs(a - 1) < 1e-12 else (re * a, im * a)
    if abs(a) < 1e-12:
        return (im * -b, re * b) if abs(abs(b) - 1) > 1e-12 else ((-im, re) if b > 0 else (im, -re))
    if abs(abs(a) - abs(b)) < 1e-12:
        if a * b > 0:
            return ((re - im) * a, (re + im) * a)
        return ((re + im) * a, (im - re) * a)
    return (re * a - im * b, re * b + im * a)


def small_dft(values, sign):
    count = len(values)
    if count == 1:
        return values
    even, odd = small_dft(values[0::2], sign), small_dft(values[1::2], sign)
    low, high = [], []
    for k in range(count // 2):
        turned = times_const(odd[k], np.exp(sign * 2j * math.pi * k / count))
        low.append((even[k][0] + turned[0], even[k][1] + turned[1]))
        high.append((even[k][0] - turned[0], even[k][1] - turned[1]))
    return low + high


def factors(total):
    bits = total.bit_length() - 1
    return 1 << (bits // 2), total // (1 << (bits // 2))


def stage_one(values, n0, count, sign, keep):
    width = len(values)
    for k1, value in enumerate(small_dft(values, sign)):
        re, im = times_const(value, np.exp(sign * 2j * math.pi * n0 * k1 / count))
        keep[n0 * width + k1, 0] = re
        keep[n0 * width + k1, 1] = im


def stage_two(k1, width, count, sign, keep):
    values = [(keep[n0 * width + k1, 0], keep[n0 * width + k1, 1]) for n0 in range(count // width)]
    return small_dft(values, sign)


def pair(ref, z):
    return ref[0, z, 0], ref[0, z, 1]


def put(ref, z, value):
    ref[0, z, 0] = value[0]
    ref[0, z, 1] = value[1]


def returned(refs, z):
    place, plane = divmod(z, sum(ref.shape[1] for ref in refs))
    for ref in refs:
        if plane < ref.shape[1]:
            return ref[place, plane, 0, 0], ref[place, plane, 1, 0]
        plane -= ref.shape[1]


def invert_one(refs, depth, width, rest, keep):
    for n0 in range(rest):
        stage_one([returned(refs, n0 + rest * n1) for n1 in range(width)], n0, depth, 1, keep)


def finish(spec, depth, rest, keep, *at):
    for j1 in range(rest):
        for j0, (re, im) in enumerate(stage_two(j1, rest, depth, -1, keep)):
            spec[(j1 + rest * j0, *at, 0)] = re
            spec[(j1 + rest * j0, *at, 1)] = im


def start_kernel(chi, inc, source, spec, keep):
    depth = inc.shape[1]
    width, rest = factors(depth)
    for n0 in range(width):
        values = []
        for n1 in range(rest):
            z = n0 + width * n1
            cr, ci = chi[0, z], chi[1, z]
            er, ei = pair(inc, z)
            w = (cr * er - ci * ei, cr * ei + ci * er)
            put(source, z, w)
            values.append(w)
        stage_one(values, n0, depth, -1, keep)
    finish(spec, depth, rest, keep)


def adjoint_kernel(first, scal, chi, inc, source, data, *refs):
    if first:
        *fields, scat_out, spec, keep_in, keep, keep_resid = refs
    else:
        field, spec, keep, keep_resid = refs
    depth = inc.shape[1]
    width, rest = factors(depth)
    object_weight, data_weight = scal[0, 0], scal[0, 1]
    if first:
        invert_one(fields, depth, width, rest, keep_in)
    for k1 in range(width):
        scattered = stage_two(k1, width, depth, 1, keep_in) if first else None
        values, resid = [], []
        for k0 in range(rest):
            z = k1 + width * k0
            if first:
                sr, si = scattered[k0]
                put(scat_out, z, (sr, si))
            else:
                sr, si = pair(field, z)
            cr, ci = chi[0, z], chi[1, z]
            er, ei = pair(inc, z)
            wr, wi = pair(source, z)
            ur, ui = er + sr, ei + si
            rr = object_weight * (cr * ur - ci * ui - wr)
            ri = object_weight * (cr * ui + ci * ur - wi)
            vr = -(cr * rr + ci * ri)
            vi = ci * rr - cr * ri
            if z == 0:
                vr = vr + data_weight * (data[0, 0] - sr)
                vi = vi + data_weight * (data[0, 1] - si)
            values.append((vr, vi))
            resid.append((rr, ri))
        stage_one(values, k1, depth, -1, keep)
        stage_one(resid, k1, depth, -1, keep_resid)
    finish(spec, depth, rest, keep, 0)
    finish(spec, depth, rest, keep_resid, 1)


def descent_kernel(*refs):
    *fields, descent, sums, keep_in = refs
    depth = descent.shape[1]
    width, rest = factors(depth)
    invert_one(fields, depth, width, rest, keep_in)
    total = jnp.zeros(sums.shape[3:], F32)
    for k1 in range(width):
        for k0, (dr, di) in enumerate(stage_two(k1, width, depth, 1, keep_in)):
            put(descent, k1 + width * k0, (dr, di))
            total = total + (dr * dr + di * di)
    sums[0, 0, 0] = total


def image_kernel(descent, chi, *refs):
    *fields, image, sums, keep_in = refs
    depth = descent.shape[1]
    width, rest = factors(depth)
    invert_one(fields, depth, width, rest, keep_in)
    change = plane = jnp.zeros(sums.shape[3:], F32)
    for k1 in range(width):
        for k0, (hr, hi) in enumerate(stage_two(k1, width, depth, 1, keep_in)):
            z = k1 + width * k0
            put(image, z, (hr, hi))
            dr, di = pair(descent, z)
            cr, ci = chi[0, z], chi[1, z]
            qr = dr - (cr * hr - ci * hi)
            qi = di - (cr * hi + ci * hr)
            change = change + (qr * qr + qi * qi)
            if z == 0:
                plane = hr * hr + hi * hi
    sums[0, 0, 0] = change
    sums[0, 0, 1] = plane


def step_kernel(last, scal, source, descent, scattered, image, inc, source_out, *rest_refs):
    if last:
        (parts,) = rest_refs
    else:
        scat_out, parts = rest_refs
    sources, depth = inc.shape[:2]
    step = scal[0, 0]

    def body(z, _):
        nr = ni = power = None
        for s in range(sources):
            dr, di = descent[s, z, 0], descent[s, z, 1]
            wr, wi = source[s, z, 0] + step * dr, source[s, z, 1] + step * di
            source_out[s, z, 0] = wr
            source_out[s, z, 1] = wi
            sr = scattered[s, z, 0] + step * image[s, z, 0]
            si = scattered[s, z, 1] + step * image[s, z, 1]
            if not last:
                scat_out[s, z, 0] = sr
                scat_out[s, z, 1] = si
            ur, ui = inc[s, z, 0] + sr, inc[s, z, 1] + si
            a, b, c = wr * ur + wi * ui, wi * ur - wr * ui, ur * ur + ui * ui
            nr, ni, power = (a, b, c) if s == 0 else (nr + a, ni + b, power + c)
        parts[0, z] = nr
        parts[1, z] = ni
        parts[2, z] = power
        return 0

    lax.fori_loop(0, depth, body, 0, unroll=4)


def assemble_kernel(spot, *refs):
    *rounds, out = refs
    turn = lax.rem(spot[0] + len(rounds) - pl.program_id(0), len(rounds))
    for t, ref in enumerate(rounds):

        @pl.when(turn == t)
        def _(ref=ref):
            for z in range(out.shape[2]):
                out[:, 0, z] = ref[:, z, 0]
                out[:, 1, z] = ref[:, z, 1]


def half_tables(total, order):
    half = total // 2
    modes = np.arange(half)[:, None]
    place = np.asarray(order)[None, :]
    out = []
    for odd in (0, 1):
        angle = 2.0 * math.pi * ((2 * modes + odd) * place % total) / total
        cosine, sine = np.cos(angle), np.sin(angle)
        out.append(np.block([[cosine, sine], [-sine, cosine]]).astype(np.float32))
    return np.stack(out)


def high_low(table):
    high = table.astype(ml_dtypes.bfloat16)
    low = (table - high.astype(np.float32)).astype(ml_dtypes.bfloat16)
    return np.stack([high, low])


def lateral_modes(total):
    index = np.concatenate([np.arange(0, total, 2), np.arange(1, total, 2)])
    return (4.0 * np.sin(math.pi * index / total) ** 2).astype(np.float32)


def split(value):
    high = value.astype(jnp.bfloat16)
    return high, (value - high.astype(F32)).astype(jnp.bfloat16)


def left_mul(table, odd, value):
    high, low = split(value)
    return jnp.dot(
        jnp.concatenate([table[0, odd], table[0, odd], table[1, odd]], axis=1),
        jnp.concatenate([high, low, high], axis=0),
        preferred_element_type=F32,
    )


def right_mul(value, table, odd):
    high, low = split(value)
    return jnp.dot(
        jnp.concatenate([high, low, high], axis=1),
        jnp.concatenate([table[0, odd], table[0, odd], table[1, odd]], axis=0),
        preferred_element_type=F32,
    )


def lateral(own, other, xf, yf):
    hx, ny = own[0].shape
    hy = ny // 2
    across = [
        left_mul(xf, 0, jnp.concatenate([own[0] + other[0], own[1] + other[1]], axis=0)),
        left_mul(xf, 1, jnp.concatenate([own[0] - other[0], own[1] - other[1]], axis=0)),
    ]
    real = jnp.concatenate([across[0][:hx], across[1][:hx]], axis=0)
    imag = jnp.concatenate([across[0][hx:], across[1][hx:]], axis=0)
    spectra = []
    for odd in (0, 1):
        flip = -1.0 if odd else 1.0
        folded = jnp.concatenate(
            [real[:, :hy] + flip * real[:, hy:], imag[:, :hy] + flip * imag[:, hy:]], axis=1
        )
        freq = right_mul(folded, yf, odd)
        spectra.append((freq[:, :hy], freq[:, hy:]))
    return spectra


def lateral_back(spectra, xb, yb, out):
    back = [right_mul(jnp.concatenate(spectra[odd], axis=1), yb, odd) for odd in (0, 1)]
    senders, _, _, _, rows, ny = out.shape
    hx, hy = senders * rows, ny // 2
    plus, minus = back[0] + back[1], back[0] - back[1]
    real = jnp.concatenate([plus[:, :hy], minus[:, :hy]], axis=1)
    imag = jnp.concatenate([plus[:, hy:], minus[:, hy:]], axis=1)
    even = left_mul(xb, 0, jnp.concatenate([real[:hx], imag[:hx]], axis=0))
    odd = left_mul(xb, 1, jnp.concatenate([real[hx:], imag[hx:]], axis=0))
    plus, minus = even + odd, even - odd
    for c in (0, 1):
        out[:, 0, c, 0] = plus[c * hx : (c + 1) * hx].reshape(senders, rows, ny)
        out[:, 0, c, 1] = minus[c * hx : (c + 1) * hx].reshape(senders, rows, ny)


def filtered(value, sign, scale, lz, lx, ly, odd):
    wave_sq = WAVENUMBER * WAVENUMBER
    eigen = (lx[...] + lz[pl.program_id(0)]) + ly[odd]
    real_den = eigen - wave_sq
    imag_den = wave_sq * DAMPING
    factor = (wave_sq * scale) / (real_den * real_den + imag_den * imag_den)
    gr, gi = factor * real_den, factor * (imag_den * sign)
    fr, fi = value
    return fr * gr - fi * gi, fr * gi + fi * gr


def loaded(ref, *at):
    return [ref[(slice(None), 0, *at, c)].reshape(-1, ref.shape[-1]) for c in (0, 1)]


def plane_kernel(scale, lz, lx, ly, xf, xb, yf, yb, own, other, out):
    spectra = lateral(loaded(own), loaded(other), xf, yf)
    lateral_back([filtered(spectra[odd], 1.0, scale, lz, lx, ly, odd) for odd in (0, 1)], xb, yb, out)


def adjoint_plane_kernel(scale, lz, lx, ly, xf, xb, yf, yb, own, other, out, keep):
    inner = lateral(loaded(own, 0), loaded(other, 0), xf, yf)
    resid = lateral(loaded(own, 1), loaded(other, 1), xf, yf)
    spectra = []
    for odd in (0, 1):
        re, im = filtered(inner[odd], -1.0, scale, lz, lx, ly, odd)
        re, im = re + scale * resid[odd][0], im + scale * resid[odd][1]
        keep[0, odd, 0], keep[0, odd, 1] = re, im
        spectra.append((re, im))
    lateral_back(spectra, xb, yb, out)


def image_plane_kernel(lz, lx, ly, xb, yb, kept, out):
    spectra = [
        filtered((kept[0, odd, 0], kept[0, odd, 1]), 1.0, 1.0, lz, lx, ly, odd) for odd in (0, 1)
    ]
    lateral_back(spectra, xb, yb, out)


SMEM = pl.BlockSpec(memory_space=pltpu.SMEM)


class Slabs:
    def __init__(self, sources, depth, rows, ny, pieces):
        self.sources, self.depth, self.rows, self.ny, self.pieces = sources, depth, rows, ny, pieces
        self.lanes = 128 if ny % 128 == 0 else ny
        self.deep = depth // 4 if depth % 4 == 0 else depth

    def kind(self, name, chunk):
        s, z, q, y, lanes, deep = self.sources, self.depth, self.rows, self.ny, self.lanes, self.deep
        turns = (y // lanes, s)
        if name.startswith("piece"):
            count = self.pieces[int(name[5:])]
            owners = z // sum(self.pieces)
            return (
                (s * owners, count, 2, 2, q, y),
                (owners, count, 2, 1, q, lanes),
                lambda j, i: (i, 0, 0, chunk, 0, j),
            )
        return {
            "field": ((s, z, 2, q, y), (1, z, 2, q, lanes), lambda j, i: (i, 0, 0, 0, j)),
            "spec": ((s * z, 2, q, y), (z, 2, q, lanes), lambda j, i: (i, 0, 0, j)),
            "twin": ((s * z, 2, 2, q, y), (z, 2, 2, q, lanes), lambda j, i: (i, 0, 0, 0, j)),
            "chi": ((2, z, q, y), (2, z, q, lanes), lambda j, i: (0, 0, 0, j)),
            "data": ((s, 2, q, y), (1, 2, q, lanes), lambda j, i: (i, 0, 0, j)),
            "sum1": (turns + (1, q, lanes), (1, 1, 1, q, lanes), lambda j, i: (j, i, 0, 0, 0)),
            "sum2": (turns + (2, q, lanes), (1, 1, 2, q, lanes), lambda j, i: (j, i, 0, 0, 0)),
            "every": ((s, z, 2, q, y), (s, deep, 2, q, lanes), lambda j, i: (0, i, 0, 0, j)),
            "parts": ((3, z, q, y), (3, deep, q, lanes), lambda j, i: (0, i, 0, j)),
        }[name]

    def call(self, kernel, chunk, ins, outs, scratch, *args):
        def spec(kind):
            if kind == "scal":
                return SMEM
            _, block, index = self.kind(kind, chunk)
            return pl.BlockSpec(block, index)

        sizes = [math.prod(self.kind(k, chunk)[0]) * 4 for k in (*ins, *outs) if k != "scal"]
        moved = sum(sizes)
        second = self.depth // self.deep if "parts" in outs else self.sources
        return pl.pallas_call(
            kernel,
            grid=(self.ny // self.lanes, second),
            in_specs=[spec(k) for k in ins],
            out_specs=[spec(k) for k in outs],
            out_shape=[jax.ShapeDtypeStruct(self.kind(k, chunk)[0], F32) for k in outs],
            scratch_shapes=[pltpu.VMEM((self.depth, 2, self.rows, self.lanes), F32)] * scratch,
            cost_estimate=pl.CostEstimate(flops=moved * 4, bytes_accessed=moved, transcendentals=0),
        )(*args)

    def piece_kinds(self):
        return tuple("piece%d" % m for m in range(len(self.pieces)))


def plane_call(kernel, senders, lz, tables, ins, work, rows, ny, kept_in=None, keeps=False):
    planes = lz.shape[0]
    dense = rows % 8 != 0
    lead, deep = (1, senders * rows) if dense else (senders, rows)

    def shaped(value):
        inner = value.shape[1:-2]
        value = value.reshape((senders, planes) + value.shape[1:])
        if dense:
            value = jnp.moveaxis(value, 0, -3).reshape((1, planes) + inner + (deep, ny))
        return value

    ins = [shaped(v) for v in ins]
    nx = 2 * senders * rows
    whole = lambda t: pl.BlockSpec(t.shape, lambda i, n=t.ndim: (0,) * n)
    plane = lambda shape: pl.BlockSpec(
        (shape[0], 1) + tuple(shape[2:]), lambda i, n=len(shape): (0, i) + (0,) * (n - 2)
    )
    kept = (planes, 2, 2, nx, ny // 2)
    kept_spec = pl.BlockSpec((1,) + kept[1:], lambda i: (i, 0, 0, 0, 0))
    out_shape = (lead, planes, 2, 2, deep, ny)
    shapes, specs = [jax.ShapeDtypeStruct(out_shape, F32)], [plane(out_shape)]
    if keeps:
        shapes.append(jax.ShapeDtypeStruct(kept, F32))
        specs.append(kept_spec)
    result = pl.pallas_call(
        kernel,
        grid=(planes,),
        in_specs=[SMEM] + [whole(t) for t in tables] + [plane(v.shape) for v in ins]
        + ([kept_spec] if kept_in is not None else []),
        out_specs=specs,
        out_shape=shapes,
        cost_estimate=pl.CostEstimate(
            flops=planes * work * 3 * nx * nx * ny * 2,
            bytes_accessed=work * math.prod(out_shape),
            transcendentals=0,
        ),
    )(lz, *tables, *ins, *([kept_in] if kept_in is not None else []))
    out = result[0]
    if dense:
        out = jnp.moveaxis(out.reshape((planes, 2, 2, senders, rows, ny)), 3, 0)
    return (out, result[1]) if keeps else out


def everyone(values):
    count = math.prod(lax.axis_size(name) for name in ALL)
    row = jnp.zeros((128,), F32).at[: len(values)].set(jnp.stack(values))
    sent = jnp.broadcast_to(row[None], (count, 128))
    return jnp.sum(lax.all_to_all(sent, ALL, 0, 0, tiled=True), axis=0)


def swap_halves(value):
    return lax.ppermute(value, "half", [(0, 1), (1, 0)])


def after(value, *others):
    return lax.optimization_barrier((value, *others))[0]


def bounded(numer_real, numer_imag, power, total_sources):
    floored = jnp.maximum(power, FLOOR_SHARE * total_sources)
    return jnp.stack(
        [
            jnp.clip(numer_real / floored, REAL_LOW, REAL_HIGH),
            jnp.clip(numer_imag / floored, 0.0, IMAG_HIGH),
        ]
    )


def payloads(chunks, shares, per_share, share):
    sent = []
    for t in range(shares):
        number = lax.rem(share + t, shares)
        cut = [lax.dynamic_slice_in_dim(w, number // 2 * per_share, per_share, axis=0) for w in chunks]
        sent.append(jnp.where(number % 2 == 0, cut[0], cut[1]))
    return sent


def deliver(sent, shares, per_share, share, half, gate):
    slots = shares // 2
    rounds = []
    for t in range(shares):
        pairs = []
        for a in range(shares):
            g, c = divmod((a + t) % shares, 2)
            for h in (0, 1):
                pairs.append((a * 2 + h, (h * slots + g) * 2 + (h + c) % 2))
        rounds.append(lax.ppermute(sent[t], ("src", "half"), pairs))
    spot = after(2 * lax.rem(share, slots) + lax.rem(half + share // slots, 2), gate)
    _, depth, _, rows, ny = rounds[0].shape
    whole = pl.BlockSpec(rounds[0].shape, lambda a: (0, 0, 0, 0, 0))
    out = pl.pallas_call(
        assemble_kernel,
        grid=(shares,),
        in_specs=[SMEM] + [whole] * shares,
        out_specs=pl.BlockSpec((per_share, 2, depth, None, rows, ny), lambda a: (0, 0, 0, a, 0, 0)),
        out_shape=jax.ShapeDtypeStruct((per_share, 2, depth, shares, rows, ny), F32),
        name="assemble",
    )(spot.reshape(1).astype(jnp.int32), *rounds)
    return out.reshape(per_share, 2, depth, shares * rows, ny)


def on_device(contrast, measured, positions):
    shares, rest_count = lax.axis_size("src"), lax.axis_size("rest")
    share, half, rest = (lax.axis_index(name) for name in ALL)
    senders = shares * rest_count
    _, depth, block_rows, ny = contrast.shape
    rows = block_rows // shares
    nx = block_rows * 2 * rest_count
    per_share = positions.shape[0]
    total_sources = per_share * shares
    sources = total_sources // 2
    planes = sources * depth // senders
    slabs = Slabs(sources, depth, rows, ny, (planes,))

    chi_own = lax.dynamic_index_in_dim(
        contrast.reshape(2, depth, shares, rows, ny), share, axis=2, keepdims=False
    )
    chi = [chi_own, swap_halves(chi_own)]

    spots = jnp.pad(positions.astype(F32).reshape(1, -1), ((0, 0), (0, 126)))
    sent = jnp.concatenate(
        [
            measured.reshape(per_share, 2, shares, rows * ny).transpose(2, 0, 1, 3).reshape(shares, -1),
            jnp.broadcast_to(spots, (shares, spots.shape[1])),
        ],
        axis=1,
    )
    got = lax.all_to_all(sent, "src", 0, 0, tiled=True)
    cells = per_share * 2 * rows * ny
    data_own = got[:, :cells].reshape(total_sources, 2, rows, ny)
    spots = got[:, cells : cells + 2 * per_share].reshape(total_sources, 2)
    mine = lambda v, h: lax.dynamic_slice_in_dim(v, h * sources, sources, axis=0)
    data = [mine(data_own, half), swap_halves(mine(data_own, 1 - half))]
    spots = mine(spots, half)

    heights = jnp.arange(depth).astype(F32) + SOURCE_GAP
    offset_y = jnp.arange(ny).astype(F32)[None] - spots[:, 1][:, None]
    inc = []
    for where in (half, 1 - half):
        start = (where * rest_count + rest) * block_rows + share * rows
        offset_x = (start + jnp.arange(rows)).astype(F32)[None] - spots[:, 0][:, None]
        dist_sq = (heights * heights)[None, :, None, None] + (offset_x * offset_x)[:, None, :, None]
        dist_sq = dist_sq + (offset_y * offset_y)[:, None, None, :]
        phases = WAVENUMBER * jnp.sqrt(dist_sq)
        inc.append(jnp.stack([jnp.cos(phases), jnp.sin(phases)], axis=2))

    order = [(k * shares + a) * rows + q for a in range(shares) for k in range(rest_count) for q in range(rows)]
    x_table, y_table = half_tables(nx, order), half_tables(ny, range(ny // 2))
    flip = lambda t: high_low(np.swapaxes(t, -1, -2))
    lx = np.broadcast_to(lateral_modes(nx)[:, None], (nx, ny // 2))
    ly = lateral_modes(ny).reshape(2, 1, ny // 2)
    lx, ly, xf, xb, yf, yb = (
        jnp.asarray(t) for t in (lx, ly, high_low(x_table), flip(x_table), flip(y_table), high_low(y_table))
    )
    place = share * rest_count + rest
    modes = (place * planes + jnp.arange(planes)) % depth
    half_sine = jnp.sin(math.pi * modes.astype(F32) / depth)
    lz = 4.0 * half_sine * half_sine
    scale = 1.0 / (nx * ny * depth)

    def exchange(value):
        flat = value.reshape((senders * planes,) + value.shape[-4:])
        return lax.all_to_all(flat, GROUP, 0, 0, tiled=True).reshape(value.shape)

    call_planes = lambda kernel, tables, ins, work, **kw: plane_call(
        kernel, senders, lz, tables, ins, work, rows, ny, **kw
    )
    tables = (lx, ly, xf, xb, yf, yb)

    both = (0, 1)
    piece_kinds = slabs.piece_kinds()
    totals = everyone([jnp.sum(measured * measured), total_sources * jnp.sum(chi_own * chi_own)])
    data_weight = 1.0 / totals[0]
    object_total = totals[1]
    source, came = [None, None], [None, None]
    for c in both:
        source[c], spec = slabs.call(start_kernel, c, ("chi", "field"), ("field", "spec"), 1, chi[c], inc[c])
        came[c] = lax.all_to_all(spec, GROUP, 0, 0, tiled=True)
    fields = exchange(call_planes(partial(plane_kernel, scale), tables, came, 8))
    scattered = [None, None]
    for outer in range(OUTER):
        object_weight = 1.0 / object_total
        weights = jnp.stack([object_weight, data_weight]).reshape(1, 2)
        first, last = outer == 0, outer == OUTER - 1
        descent, image, came = [None, None], [None, None], [None, None]
        for c in both:
            out = slabs.call(
                partial(adjoint_kernel, first),
                c,
                ("scal", "chi", "field", "field", "data") + (piece_kinds if first else ("field",)),
                ("field", "twin") if first else ("twin",),
                3 if first else 2,
                weights, chi[c], inc[c], source[c], data[c], *((fields,) if first else (scattered[c],)),
            )
            if first:
                scattered[c] = out[0]
            came[c] = lax.all_to_all(out[-1], GROUP, 0, 0, tiled=True)
        part, kept = call_planes(partial(adjoint_plane_kernel, scale), tables, came, 12, keeps=True)
        fields = exchange(part)
        fields_image = exchange(call_planes(image_plane_kernel, (lx, ly, xb, yb), [], 4, kept_in=kept))
        sums = []
        for c in both:
            descent[c], part = slabs.call(descent_kernel, c, piece_kinds, ("field", "sum1"), 1, fields)
            sums.append(part)
        sum_d = jnp.sum(sums[0]) + jnp.sum(sums[1])
        sums = []
        for c in both:
            image[c], part = slabs.call(
                image_kernel, c, ("field", "chi") + piece_kinds, ("field", "sum2"), 1,
                descent[c], chi[c], fields_image,
            )
            sums.append(part)
        sum_q = sums[0] + sums[1]
        totals = everyone([sum_d, jnp.sum(sum_q[:, :, 0]), jnp.sum(sum_q[:, :, 1])])
        step = totals[0] / (data_weight * totals[2] + object_weight * totals[1])
        parts = [None, None]
        for c in (1, 0):
            out = slabs.call(
                partial(step_kernel, last),
                c,
                ("scal",) + ("every",) * 5,
                ("every",) * (1 if last else 2) + ("parts",),
                0,
                step.reshape(1, 1), source[c], descent[c], scattered[c], image[c], inc[c],
            )
            source[c], parts[c] = out[0], out[-1]
            if not last:
                scattered[c] = out[1]
        received = swap_halves(parts[1])
        if last:
            sent = payloads(source, shares, per_share, share)
            received, *sent = lax.optimization_barrier((received, *sent))
        sums = parts[0] + received
        chi_own = bounded(sums[0], sums[1], sums[2], total_sources)
        if not last:
            object_total = everyone([total_sources * jnp.sum(chi_own * chi_own)])[0]
            chi = [chi_own, swap_halves(after(chi_own, object_total))]

    copies = jnp.broadcast_to(chi_own[None], (shares,) + chi_own.shape)
    contrast_new = lax.all_to_all(copies, "src", 0, 0, tiled=True)
    contrast_new = contrast_new.transpose(1, 2, 0, 3, 4).reshape(contrast.shape)
    contrast_sources = deliver(sent, shares, per_share, share, half, contrast_new)
    return contrast_sources, contrast_new


def solution(mesh):
    shares, spaces = mesh.shape["src"], mesh.shape["space"]
    split_mesh = Mesh(mesh.devices.reshape(shares, 2, spaces // 2), ALL)
    space = ("half", "rest")

    return jax.shard_map(
        on_device,
        mesh=split_mesh,
        in_specs=(P(None, None, space, None), P("src", None, space, None), P("src", None)),
        out_specs=(P("src", None, None, space, None), P(None, None, space, None)),
        check_vma=False,
    )
```

```python
from functools import partial
import math

import jax
import jax.numpy as jnp
import ml_dtypes
import numpy as np
from jax import lax
from jax.experimental import pallas as pl
from jax.experimental.pallas import tpu as pltpu
from jax.sharding import Mesh, PartitionSpec as P


OUTER = 2
WAVENUMBER = 2.0 * math.pi / 6.0
DAMPING = 0.3
SOURCE_GAP = 8.0
FLOOR_SHARE = 0.75
REAL_LOW = -0.25
REAL_HIGH = 0.35
IMAG_HIGH = 0.1
ALL = ("src", "half", "rest")
GROUP = ("src", "rest")
F32 = jnp.float32


def times_const(value, factor):
    re, im = value
    a, b = factor.real, factor.imag
    if abs(b) < 1e-12:
        return (re, im) if abs(a - 1) < 1e-12 else (re * a, im * a)
    if abs(a) < 1e-12:
        return (im * -b, re * b) if abs(abs(b) - 1) > 1e-12 else ((-im, re) if b > 0 else (im, -re))
    if abs(abs(a) - abs(b)) < 1e-12:
        if a * b > 0:
            return ((re - im) * a, (re + im) * a)
        return ((re + im) * a, (im - re) * a)
    return (re * a - im * b, re * b + im * a)


def small_dft(values, sign):
    count = len(values)
    if count == 1:
        return values
    even, odd = small_dft(values[0::2], sign), small_dft(values[1::2], sign)
    low, high = [], []
    for k in range(count // 2):
        turned = times_const(odd[k], np.exp(sign * 2j * math.pi * k / count))
        low.append((even[k][0] + turned[0], even[k][1] + turned[1]))
        high.append((even[k][0] - turned[0], even[k][1] - turned[1]))
    return low + high


def factors(total):
    bits = total.bit_length() - 1
    return 1 << (bits // 2), total // (1 << (bits // 2))


def stage_one(values, n0, count, sign, keep):
    width = len(values)
    for k1, value in enumerate(small_dft(values, sign)):
        re, im = times_const(value, np.exp(sign * 2j * math.pi * n0 * k1 / count))
        keep[n0 * width + k1, 0] = re
        keep[n0 * width + k1, 1] = im


def stage_two(k1, width, count, sign, keep):
    values = [(keep[n0 * width + k1, 0], keep[n0 * width + k1, 1]) for n0 in range(count // width)]
    return small_dft(values, sign)


def pair(ref, z):
    return ref[0, z, 0], ref[0, z, 1]


def put(ref, z, value):
    ref[0, z, 0] = value[0]
    ref[0, z, 1] = value[1]


def returned(refs, z):
    place, plane = divmod(z, sum(ref.shape[1] for ref in refs))
    for ref in refs:
        if plane < ref.shape[1]:
            return ref[place, plane, 0, 0], ref[place, plane, 1, 0]
        plane -= ref.shape[1]


def invert_one(refs, depth, width, rest, keep):
    for n0 in range(rest):
        stage_one([returned(refs, n0 + rest * n1) for n1 in range(width)], n0, depth, 1, keep)


def finish(spec, depth, rest, keep, *at):
    for j1 in range(rest):
        for j0, (re, im) in enumerate(stage_two(j1, rest, depth, -1, keep)):
            spec[(j1 + rest * j0, *at, 0)] = re
            spec[(j1 + rest * j0, *at, 1)] = im


def start_kernel(chi, inc, source, spec, keep):
    depth = inc.shape[1]
    width, rest = factors(depth)
    for n0 in range(width):
        values = []
        for n1 in range(rest):
            z = n0 + width * n1
            cr, ci = chi[0, z], chi[1, z]
            er, ei = pair(inc, z)
            w = (cr * er - ci * ei, cr * ei + ci * er)
            put(source, z, w)
            values.append(w)
        stage_one(values, n0, depth, -1, keep)
    finish(spec, depth, rest, keep)


def adjoint_kernel(first, scal, chi, source, data, field, *refs):
    if first:
        *fields, total_out, spec, keep_in, keep, keep_resid = refs
    else:
        spec, keep, keep_resid = refs
    depth = source.shape[1]
    width, rest = factors(depth)
    object_weight, data_weight = scal[0, 0], scal[0, 1]
    if first:
        invert_one(fields, depth, width, rest, keep_in)
    for k1 in range(width):
        scattered = stage_two(k1, width, depth, 1, keep_in) if first else None
        values, resid = [], []
        for k0 in range(rest):
            z = k1 + width * k0
            ur, ui = pair(field, z)
            if first:
                ur, ui = ur + scattered[k0][0], ui + scattered[k0][1]
                put(total_out, z, (ur, ui))
            cr, ci = chi[0, z], chi[1, z]
            wr, wi = pair(source, z)
            rr = object_weight * (cr * ur - ci * ui - wr)
            ri = object_weight * (cr * ui + ci * ur - wi)
            vr = -(cr * rr + ci * ri)
            vi = ci * rr - cr * ri
            if z == 0:
                vr = vr + data_weight * (data[0, 0] - ur)
                vi = vi + data_weight * (data[0, 1] - ui)
            values.append((vr, vi))
            resid.append((rr, ri))
        stage_one(values, k1, depth, -1, keep)
        stage_one(resid, k1, depth, -1, keep_resid)
    finish(spec, depth, rest, keep, 0)
    finish(spec, depth, rest, keep_resid, 1)


def descent_kernel(*refs):
    *fields, descent, sums, keep_in = refs
    depth = descent.shape[1]
    width, rest = factors(depth)
    invert_one(fields, depth, width, rest, keep_in)
    total = jnp.zeros(sums.shape[3:], F32)
    for k1 in range(width):
        for k0, (dr, di) in enumerate(stage_two(k1, width, depth, 1, keep_in)):
            put(descent, k1 + width * k0, (dr, di))
            total = total + (dr * dr + di * di)
    sums[0, 0, 0] = total


def image_kernel(descent, chi, *refs):
    *fields, image, sums, keep_in = refs
    depth = descent.shape[1]
    width, rest = factors(depth)
    invert_one(fields, depth, width, rest, keep_in)
    change = plane = jnp.zeros(sums.shape[3:], F32)
    for k1 in range(width):
        for k0, (hr, hi) in enumerate(stage_two(k1, width, depth, 1, keep_in)):
            z = k1 + width * k0
            put(image, z, (hr, hi))
            dr, di = pair(descent, z)
            cr, ci = chi[0, z], chi[1, z]
            qr = dr - (cr * hr - ci * hi)
            qi = di - (cr * hi + ci * hr)
            change = change + (qr * qr + qi * qi)
            if z == 0:
                plane = hr * hr + hi * hi
    sums[0, 0, 0] = change
    sums[0, 0, 1] = plane


def step_kernel(last, scal, source, descent, field, image, source_out, *rest_refs):
    if last:
        (parts,) = rest_refs
    else:
        field_out, parts = rest_refs
    sources, depth = source.shape[:2]
    step = scal[0, 0]

    def body(z, _):
        nr = ni = power = None
        for s in range(sources):
            dr, di = descent[s, z, 0], descent[s, z, 1]
            wr, wi = source[s, z, 0] + step * dr, source[s, z, 1] + step * di
            source_out[s, z, 0] = wr
            source_out[s, z, 1] = wi
            ur = field[s, z, 0] + step * image[s, z, 0]
            ui = field[s, z, 1] + step * image[s, z, 1]
            if not last:
                field_out[s, z, 0] = ur
                field_out[s, z, 1] = ui
            a, b, c = wr * ur + wi * ui, wi * ur - wr * ui, ur * ur + ui * ui
            nr, ni, power = (a, b, c) if s == 0 else (nr + a, ni + b, power + c)
        parts[0, z] = nr
        parts[1, z] = ni
        parts[2, z] = power
        return 0

    lax.fori_loop(0, depth, body, 0, unroll=4)


def assemble_kernel(spot, *refs):
    *rounds, out = refs
    turn = lax.rem(spot[0] + len(rounds) - pl.program_id(0), len(rounds))
    for t, ref in enumerate(rounds):

        @pl.when(turn == t)
        def _(ref=ref):
            for z in range(out.shape[2]):
                out[:, 0, z] = ref[:, z, 0]
                out[:, 1, z] = ref[:, z, 1]


def half_tables(total, order):
    half = total // 2
    modes = np.arange(half)[:, None]
    place = np.asarray(order)[None, :]
    out = []
    for odd in (0, 1):
        angle = 2.0 * math.pi * ((2 * modes + odd) * place % total) / total
        cosine, sine = np.cos(angle), np.sin(angle)
        out.append(np.block([[cosine, sine], [-sine, cosine]]).astype(np.float32))
    return np.stack(out)


def high_low(table):
    high = table.astype(ml_dtypes.bfloat16)
    low = (table - high.astype(np.float32)).astype(ml_dtypes.bfloat16)
    return np.stack([high, low])


def lateral_modes(total):
    index = np.concatenate([np.arange(0, total, 2), np.arange(1, total, 2)])
    return (4.0 * np.sin(math.pi * index / total) ** 2).astype(np.float32)


def split(value):
    high = value.astype(jnp.bfloat16)
    return high, (value - high.astype(F32)).astype(jnp.bfloat16)


def left_mul(table, odd, value):
    high, low = split(value)
    return jnp.dot(
        jnp.concatenate([table[0, odd], table[0, odd], table[1, odd]], axis=1),
        jnp.concatenate([high, low, high], axis=0),
        preferred_element_type=F32,
    )


def right_mul(value, table, odd):
    high, low = split(value)
    return jnp.dot(
        jnp.concatenate([high, low, high], axis=1),
        jnp.concatenate([table[0, odd], table[0, odd], table[1, odd]], axis=0),
        preferred_element_type=F32,
    )


def lateral(own, other, xf, yf):
    hx, ny = own[0].shape
    hy = ny // 2
    across = [
        left_mul(xf, 0, jnp.concatenate([own[0] + other[0], own[1] + other[1]], axis=0)),
        left_mul(xf, 1, jnp.concatenate([own[0] - other[0], own[1] - other[1]], axis=0)),
    ]
    real = jnp.concatenate([across[0][:hx], across[1][:hx]], axis=0)
    imag = jnp.concatenate([across[0][hx:], across[1][hx:]], axis=0)
    spectra = []
    for odd in (0, 1):
        flip = -1.0 if odd else 1.0
        folded = jnp.concatenate(
            [real[:, :hy] + flip * real[:, hy:], imag[:, :hy] + flip * imag[:, hy:]], axis=1
        )
        freq = right_mul(folded, yf, odd)
        spectra.append((freq[:, :hy], freq[:, hy:]))
    return spectra


def lateral_back(spectra, xb, yb, out):
    back = [right_mul(jnp.concatenate(spectra[odd], axis=1), yb, odd) for odd in (0, 1)]
    senders, _, _, _, rows, ny = out.shape
    hx, hy = senders * rows, ny // 2
    plus, minus = back[0] + back[1], back[0] - back[1]
    real = jnp.concatenate([plus[:, :hy], minus[:, :hy]], axis=1)
    imag = jnp.concatenate([plus[:, hy:], minus[:, hy:]], axis=1)
    even = left_mul(xb, 0, jnp.concatenate([real[:hx], imag[:hx]], axis=0))
    odd = left_mul(xb, 1, jnp.concatenate([real[hx:], imag[hx:]], axis=0))
    plus, minus = even + odd, even - odd
    for c in (0, 1):
        out[:, 0, c, 0] = plus[c * hx : (c + 1) * hx].reshape(senders, rows, ny)
        out[:, 0, c, 1] = minus[c * hx : (c + 1) * hx].reshape(senders, rows, ny)


def filtered(value, sign, scale, lz, lx, ly, odd):
    wave_sq = WAVENUMBER * WAVENUMBER
    eigen = (lx[...] + lz[pl.program_id(0)]) + ly[odd]
    real_den = eigen - wave_sq
    imag_den = wave_sq * DAMPING
    factor = (wave_sq * scale) / (real_den * real_den + imag_den * imag_den)
    gr, gi = factor * real_den, factor * (imag_den * sign)
    fr, fi = value
    return fr * gr - fi * gi, fr * gi + fi * gr


def loaded(ref, *at):
    return [ref[(slice(None), 0, *at, c)].reshape(-1, ref.shape[-1]) for c in (0, 1)]


def plane_kernel(scale, lz, lx, ly, xf, xb, yf, yb, own, other, out):
    spectra = lateral(loaded(own), loaded(other), xf, yf)
    lateral_back([filtered(spectra[odd], 1.0, scale, lz, lx, ly, odd) for odd in (0, 1)], xb, yb, out)


def adjoint_plane_kernel(scale, lz, lx, ly, xf, xb, yf, yb, own, other, out, keep):
    inner = lateral(loaded(own, 0), loaded(other, 0), xf, yf)
    resid = lateral(loaded(own, 1), loaded(other, 1), xf, yf)
    spectra = []
    for odd in (0, 1):
        re, im = filtered(inner[odd], -1.0, scale, lz, lx, ly, odd)
        re, im = re + scale * resid[odd][0], im + scale * resid[odd][1]
        keep[0, odd, 0], keep[0, odd, 1] = re, im
        spectra.append((re, im))
    lateral_back(spectra, xb, yb, out)


def image_plane_kernel(lz, lx, ly, xb, yb, kept, out):
    spectra = [
        filtered((kept[0, odd, 0], kept[0, odd, 1]), 1.0, 1.0, lz, lx, ly, odd) for odd in (0, 1)
    ]
    lateral_back(spectra, xb, yb, out)


SMEM = pl.BlockSpec(memory_space=pltpu.SMEM)


class Slabs:
    def __init__(self, sources, depth, rows, ny, pieces):
        self.sources, self.depth, self.rows, self.ny, self.pieces = sources, depth, rows, ny, pieces
        self.lanes = 128 if ny % 128 == 0 else ny
        self.deep = depth // 4 if depth % 4 == 0 else depth

    def kind(self, name, chunk):
        s, z, q, y, lanes, deep = self.sources, self.depth, self.rows, self.ny, self.lanes, self.deep
        turns = (y // lanes, s)
        if name.startswith("piece"):
            count = self.pieces[int(name[5:])]
            owners = z // sum(self.pieces)
            return (
                (s * owners, count, 2, 2, q, y),
                (owners, count, 2, 1, q, lanes),
                lambda j, i: (i, 0, 0, chunk, 0, j),
            )
        return {
            "field": ((s, z, 2, q, y), (1, z, 2, q, lanes), lambda j, i: (i, 0, 0, 0, j)),
            "spec": ((s * z, 2, q, y), (z, 2, q, lanes), lambda j, i: (i, 0, 0, j)),
            "twin": ((s * z, 2, 2, q, y), (z, 2, 2, q, lanes), lambda j, i: (i, 0, 0, 0, j)),
            "chi": ((2, z, q, y), (2, z, q, lanes), lambda j, i: (0, 0, 0, j)),
            "data": ((s, 2, q, y), (1, 2, q, lanes), lambda j, i: (i, 0, 0, j)),
            "sum1": (turns + (1, q, lanes), (1, 1, 1, q, lanes), lambda j, i: (j, i, 0, 0, 0)),
            "sum2": (turns + (2, q, lanes), (1, 1, 2, q, lanes), lambda j, i: (j, i, 0, 0, 0)),
            "every": ((s, z, 2, q, y), (s, deep, 2, q, lanes), lambda j, i: (0, i, 0, 0, j)),
            "parts": ((3, z, q, y), (3, deep, q, lanes), lambda j, i: (0, i, 0, j)),
        }[name]

    def call(self, kernel, chunk, ins, outs, scratch, *args):
        def spec(kind):
            if kind == "scal":
                return SMEM
            _, block, index = self.kind(kind, chunk)
            return pl.BlockSpec(block, index)

        sizes = [math.prod(self.kind(k, chunk)[0]) * 4 for k in (*ins, *outs) if k != "scal"]
        moved = sum(sizes)
        second = self.depth // self.deep if "parts" in outs else self.sources
        return pl.pallas_call(
            kernel,
            grid=(self.ny // self.lanes, second),
            in_specs=[spec(k) for k in ins],
            out_specs=[spec(k) for k in outs],
            out_shape=[jax.ShapeDtypeStruct(self.kind(k, chunk)[0], F32) for k in outs],
            scratch_shapes=[pltpu.VMEM((self.depth, 2, self.rows, self.lanes), F32)] * scratch,
            cost_estimate=pl.CostEstimate(flops=moved * 4, bytes_accessed=moved, transcendentals=0),
        )(*args)

    def piece_kinds(self):
        return tuple("piece%d" % m for m in range(len(self.pieces)))


def plane_call(kernel, senders, lz, tables, ins, work, rows, ny, kept_in=None, keeps=False):
    planes = lz.shape[0]
    dense = rows % 8 != 0
    lead, deep = (1, senders * rows) if dense else (senders, rows)

    def shaped(value):
        inner = value.shape[1:-2]
        value = value.reshape((senders, planes) + value.shape[1:])
        if dense:
            value = jnp.moveaxis(value, 0, -3).reshape((1, planes) + inner + (deep, ny))
        return value

    ins = [shaped(v) for v in ins]
    nx = 2 * senders * rows
    whole = lambda t: pl.BlockSpec(t.shape, lambda i, n=t.ndim: (0,) * n)
    plane = lambda shape: pl.BlockSpec(
        (shape[0], 1) + tuple(shape[2:]), lambda i, n=len(shape): (0, i) + (0,) * (n - 2)
    )
    kept = (planes, 2, 2, nx, ny // 2)
    kept_spec = pl.BlockSpec((1,) + kept[1:], lambda i: (i, 0, 0, 0, 0))
    out_shape = (lead, planes, 2, 2, deep, ny)
    shapes, specs = [jax.ShapeDtypeStruct(out_shape, F32)], [plane(out_shape)]
    if keeps:
        shapes.append(jax.ShapeDtypeStruct(kept, F32))
        specs.append(kept_spec)
    result = pl.pallas_call(
        kernel,
        grid=(planes,),
        in_specs=[SMEM] + [whole(t) for t in tables] + [plane(v.shape) for v in ins]
        + ([kept_spec] if kept_in is not None else []),
        out_specs=specs,
        out_shape=shapes,
        cost_estimate=pl.CostEstimate(
            flops=planes * work * 3 * nx * nx * ny * 2,
            bytes_accessed=work * math.prod(out_shape),
            transcendentals=0,
        ),
    )(lz, *tables, *ins, *([kept_in] if kept_in is not None else []))
    out = result[0]
    if dense:
        out = jnp.moveaxis(out.reshape((planes, 2, 2, senders, rows, ny)), 3, 0)
    return (out, result[1]) if keeps else out


def everyone(values):
    count = math.prod(lax.axis_size(name) for name in ALL)
    row = jnp.zeros((128,), F32).at[: len(values)].set(jnp.stack(values))
    sent = jnp.broadcast_to(row[None], (count, 128))
    return jnp.sum(lax.all_to_all(sent, ALL, 0, 0, tiled=True), axis=0)


def swap_halves(value):
    return lax.ppermute(value, "half", [(0, 1), (1, 0)])


def after(value, *others):
    return lax.optimization_barrier((value, *others))[0]


def bounded(numer_real, numer_imag, power, total_sources):
    floored = jnp.maximum(power, FLOOR_SHARE * total_sources)
    return jnp.stack(
        [
            jnp.clip(numer_real / floored, REAL_LOW, REAL_HIGH),
            jnp.clip(numer_imag / floored, 0.0, IMAG_HIGH),
        ]
    )


def payloads(chunks, shares, per_share, share):
    sent = []
    for t in range(shares):
        number = lax.rem(share + t, shares)
        cut = [lax.dynamic_slice_in_dim(w, number // 2 * per_share, per_share, axis=0) for w in chunks]
        sent.append(jnp.where(number % 2 == 0, cut[0], cut[1]))
    return sent


def deliver(sent, shares, per_share, share, half, gate):
    slots = shares // 2
    rounds = []
    for t in range(shares):
        pairs = []
        for a in range(shares):
            g, c = divmod((a + t) % shares, 2)
            for h in (0, 1):
                pairs.append((a * 2 + h, (h * slots + g) * 2 + (h + c) % 2))
        rounds.append(lax.ppermute(sent[t], ("src", "half"), pairs))
    spot = after(2 * lax.rem(share, slots) + lax.rem(half + share // slots, 2), gate)
    _, depth, _, rows, ny = rounds[0].shape
    whole = pl.BlockSpec(rounds[0].shape, lambda a: (0, 0, 0, 0, 0))
    out = pl.pallas_call(
        assemble_kernel,
        grid=(shares,),
        in_specs=[SMEM] + [whole] * shares,
        out_specs=pl.BlockSpec((per_share, 2, depth, None, rows, ny), lambda a: (0, 0, 0, a, 0, 0)),
        out_shape=jax.ShapeDtypeStruct((per_share, 2, depth, shares, rows, ny), F32),
        name="assemble",
    )(spot.reshape(1).astype(jnp.int32), *rounds)
    return out.reshape(per_share, 2, depth, shares * rows, ny)


def on_device(contrast, measured, positions):
    shares, rest_count = lax.axis_size("src"), lax.axis_size("rest")
    share, half, rest = (lax.axis_index(name) for name in ALL)
    senders = shares * rest_count
    _, depth, block_rows, ny = contrast.shape
    rows = block_rows // shares
    nx = block_rows * 2 * rest_count
    per_share = positions.shape[0]
    total_sources = per_share * shares
    sources = total_sources // 2
    planes = sources * depth // senders
    slabs = Slabs(sources, depth, rows, ny, (planes,))

    chi_own = lax.dynamic_index_in_dim(
        contrast.reshape(2, depth, shares, rows, ny), share, axis=2, keepdims=False
    )
    chi = [chi_own, swap_halves(chi_own)]

    spots = jnp.pad(positions.astype(F32).reshape(1, -1), ((0, 0), (0, 126)))
    sent = jnp.concatenate(
        [
            measured.reshape(per_share, 2, shares, rows * ny).transpose(2, 0, 1, 3).reshape(shares, -1),
            jnp.broadcast_to(spots, (shares, spots.shape[1])),
        ],
        axis=1,
    )
    got = lax.all_to_all(sent, "src", 0, 0, tiled=True)
    cells = per_share * 2 * rows * ny
    data_own = got[:, :cells].reshape(total_sources, 2, rows, ny)
    spots = got[:, cells : cells + 2 * per_share].reshape(total_sources, 2)
    mine = lambda v, h: lax.dynamic_slice_in_dim(v, h * sources, sources, axis=0)
    data = [mine(data_own, half), swap_halves(mine(data_own, 1 - half))]
    spots = mine(spots, half)

    heights = jnp.arange(depth).astype(F32) + SOURCE_GAP
    offset_y = jnp.arange(ny).astype(F32)[None] - spots[:, 1][:, None]
    inc = []
    for where in (half, 1 - half):
        start = (where * rest_count + rest) * block_rows + share * rows
        offset_x = (start + jnp.arange(rows)).astype(F32)[None] - spots[:, 0][:, None]
        dist_sq = (heights * heights)[None, :, None, None] + (offset_x * offset_x)[:, None, :, None]
        dist_sq = dist_sq + (offset_y * offset_y)[:, None, None, :]
        phases = WAVENUMBER * jnp.sqrt(dist_sq)
        inc.append(jnp.stack([jnp.cos(phases), jnp.sin(phases)], axis=2))

    order = [(k * shares + a) * rows + q for a in range(shares) for k in range(rest_count) for q in range(rows)]
    x_table, y_table = half_tables(nx, order), half_tables(ny, range(ny // 2))
    flip = lambda t: high_low(np.swapaxes(t, -1, -2))
    lx = np.broadcast_to(lateral_modes(nx)[:, None], (nx, ny // 2))
    ly = lateral_modes(ny).reshape(2, 1, ny // 2)
    lx, ly, xf, xb, yf, yb = (
        jnp.asarray(t) for t in (lx, ly, high_low(x_table), flip(x_table), flip(y_table), high_low(y_table))
    )
    place = share * rest_count + rest
    modes = (place * planes + jnp.arange(planes)) % depth
    half_sine = jnp.sin(math.pi * modes.astype(F32) / depth)
    lz = 4.0 * half_sine * half_sine
    scale = 1.0 / (nx * ny * depth)

    def exchange(value):
        flat = value.reshape((senders * planes,) + value.shape[-4:])
        return lax.all_to_all(flat, GROUP, 0, 0, tiled=True).reshape(value.shape)

    call_planes = lambda kernel, tables, ins, work, **kw: plane_call(
        kernel, senders, lz, tables, ins, work, rows, ny, **kw
    )
    tables = (lx, ly, xf, xb, yf, yb)

    both = (0, 1)
    piece_kinds = slabs.piece_kinds()
    totals = everyone([jnp.sum(measured * measured), total_sources * jnp.sum(chi_own * chi_own)])
    data_weight = 1.0 / totals[0]
    object_total = totals[1]
    source, came = [None, None], [None, None]
    for c in both:
        source[c], spec = slabs.call(start_kernel, c, ("chi", "field"), ("field", "spec"), 1, chi[c], inc[c])
        came[c] = lax.all_to_all(spec, GROUP, 0, 0, tiled=True)
    fields = exchange(call_planes(partial(plane_kernel, scale), tables, came, 8))
    total = [None, None]
    for outer in range(OUTER):
        object_weight = 1.0 / object_total
        weights = jnp.stack([object_weight, data_weight]).reshape(1, 2)
        first, last = outer == 0, outer == OUTER - 1
        descent, image, came = [None, None], [None, None], [None, None]
        for c in both:
            out = slabs.call(
                partial(adjoint_kernel, first),
                c,
                ("scal", "chi", "field", "data", "field") + (piece_kinds if first else ()),
                ("field", "twin") if first else ("twin",),
                3 if first else 2,
                weights, chi[c], source[c], data[c] + inc[c][:, 0],
                *((inc[c], fields) if first else (total[c],)),
            )
            if first:
                total[c] = out[0]
            came[c] = lax.all_to_all(out[-1], GROUP, 0, 0, tiled=True)
        part, kept = call_planes(partial(adjoint_plane_kernel, scale), tables, came, 12, keeps=True)
        fields = exchange(part)
        fields_image = exchange(call_planes(image_plane_kernel, (lx, ly, xb, yb), [], 4, kept_in=kept))
        sums = []
        for c in both:
            descent[c], part = slabs.call(descent_kernel, c, piece_kinds, ("field", "sum1"), 1, fields)
            sums.append(part)
        sum_d = jnp.sum(sums[0]) + jnp.sum(sums[1])
        sums = []
        for c in both:
            image[c], part = slabs.call(
                image_kernel, c, ("field", "chi") + piece_kinds, ("field", "sum2"), 1,
                descent[c], chi[c], fields_image,
            )
            sums.append(part)
        sum_q = sums[0] + sums[1]
        totals = everyone([sum_d, jnp.sum(sum_q[:, :, 0]), jnp.sum(sum_q[:, :, 1])])
        step = totals[0] / (data_weight * totals[2] + object_weight * totals[1])
        parts = [None, None]
        for c in (1, 0):
            out = slabs.call(
                partial(step_kernel, last),
                c,
                ("scal",) + ("every",) * 4,
                ("every",) * (1 if last else 2) + ("parts",),
                0,
                step.reshape(1, 1), source[c], descent[c], total[c], image[c],
            )
            source[c], parts[c] = out[0], out[-1]
            if not last:
                total[c] = out[1]
        received = swap_halves(parts[1])
        if last:
            sent = payloads(source, shares, per_share, share)
            received, *sent = lax.optimization_barrier((received, *sent))
        sums = parts[0] + received
        chi_own = bounded(sums[0], sums[1], sums[2], total_sources)
        if not last:
            object_total = everyone([total_sources * jnp.sum(chi_own * chi_own)])[0]
            chi = [chi_own, swap_halves(after(chi_own, object_total))]

    copies = jnp.broadcast_to(chi_own[None], (shares,) + chi_own.shape)
    contrast_new = lax.all_to_all(copies, "src", 0, 0, tiled=True)
    contrast_new = contrast_new.transpose(1, 2, 0, 3, 4).reshape(contrast.shape)
    contrast_sources = deliver(sent, shares, per_share, share, half, contrast_new)
    return contrast_sources, contrast_new


def solution(mesh):
    shares, spaces = mesh.shape["src"], mesh.shape["space"]
    split_mesh = Mesh(mesh.devices.reshape(shares, 2, spaces // 2), ALL)
    space = ("half", "rest")

    return jax.shard_map(
        on_device,
        mesh=split_mesh,
        in_specs=(P(None, None, space, None), P("src", None, space, None), P("src", None)),
        out_specs=(P("src", None, None, space, None), P(None, None, space, None)),
        check_vma=False,
    )
```

```python
from functools import partial
import math

import jax
import jax.numpy as jnp
import ml_dtypes
import numpy as np
from jax import lax
from jax.experimental import pallas as pl
from jax.experimental.pallas import tpu as pltpu
from jax.sharding import Mesh, PartitionSpec as P


OUTER = 2
WAVENUMBER = 2.0 * math.pi / 6.0
DAMPING = 0.3
SOURCE_GAP = 8.0
FLOOR_SHARE = 0.75
REAL_LOW = -0.25
REAL_HIGH = 0.35
IMAG_HIGH = 0.1
ALL = ("src", "half", "rest")
GROUP = ("src", "rest")
F32 = jnp.float32


def times_const(value, factor):
    re, im = value
    a, b = factor.real, factor.imag
    if abs(b) < 1e-12:
        return (re, im) if abs(a - 1) < 1e-12 else (re * a, im * a)
    if abs(a) < 1e-12:
        return (im * -b, re * b) if abs(abs(b) - 1) > 1e-12 else ((-im, re) if b > 0 else (im, -re))
    if abs(abs(a) - abs(b)) < 1e-12:
        if a * b > 0:
            return ((re - im) * a, (re + im) * a)
        return ((re + im) * a, (im - re) * a)
    return (re * a - im * b, re * b + im * a)


def small_dft(values, sign):
    count = len(values)
    if count == 1:
        return values
    even, odd = small_dft(values[0::2], sign), small_dft(values[1::2], sign)
    low, high = [], []
    for k in range(count // 2):
        turned = times_const(odd[k], np.exp(sign * 2j * math.pi * k / count))
        low.append((even[k][0] + turned[0], even[k][1] + turned[1]))
        high.append((even[k][0] - turned[0], even[k][1] - turned[1]))
    return low + high


def factors(total):
    bits = total.bit_length() - 1
    return 1 << (bits // 2), total // (1 << (bits // 2))


def stage_one(values, n0, count, sign, keep):
    width = len(values)
    for k1, value in enumerate(small_dft(values, sign)):
        re, im = times_const(value, np.exp(sign * 2j * math.pi * n0 * k1 / count))
        keep[n0 * width + k1, 0] = re
        keep[n0 * width + k1, 1] = im


def stage_two(k1, width, count, sign, keep):
    values = [(keep[n0 * width + k1, 0], keep[n0 * width + k1, 1]) for n0 in range(count // width)]
    return small_dft(values, sign)


def pair(ref, z):
    return ref[0, z, 0], ref[0, z, 1]


def put(ref, z, value):
    ref[0, z, 0] = value[0]
    ref[0, z, 1] = value[1]


def returned(refs, z):
    place, plane = divmod(z, sum(ref.shape[1] for ref in refs))
    for ref in refs:
        if plane < ref.shape[1]:
            return ref[place, plane, 0, 0], ref[place, plane, 1, 0]
        plane -= ref.shape[1]


def invert_one(refs, depth, width, rest, keep):
    for n0 in range(rest):
        stage_one([returned(refs, n0 + rest * n1) for n1 in range(width)], n0, depth, 1, keep)


def finish(spec, depth, rest, keep, *at):
    for j1 in range(rest):
        for j0, (re, im) in enumerate(stage_two(j1, rest, depth, -1, keep)):
            spec[(j1 + rest * j0, *at, 0)] = re
            spec[(j1 + rest * j0, *at, 1)] = im


def start_kernel(chi, inc, source, spec, keep):
    depth = inc.shape[1]
    width, rest = factors(depth)
    for n0 in range(width):
        values = []
        for n1 in range(rest):
            z = n0 + width * n1
            cr, ci = chi[0, z], chi[1, z]
            er, ei = pair(inc, z)
            w = (cr * er - ci * ei, cr * ei + ci * er)
            put(source, z, w)
            values.append(w)
        stage_one(values, n0, depth, -1, keep)
    finish(spec, depth, rest, keep)


def adjoint_kernel(first, scal, chi, source, data, field, *refs):
    if first:
        *fields, total_out, spec, keep_in, keep, keep_resid = refs
    else:
        spec, keep, keep_resid = refs
    depth = source.shape[1]
    width, rest = factors(depth)
    object_weight, data_weight = scal[0, 0], scal[0, 1]
    if first:
        invert_one(fields, depth, width, rest, keep_in)
    for k1 in range(width):
        scattered = stage_two(k1, width, depth, 1, keep_in) if first else None
        values, resid = [], []
        for k0 in range(rest):
            z = k1 + width * k0
            ur, ui = pair(field, z)
            if first:
                ur, ui = ur + scattered[k0][0], ui + scattered[k0][1]
                put(total_out, z, (ur, ui))
            cr, ci = chi[0, z], chi[1, z]
            wr, wi = pair(source, z)
            rr = object_weight * (cr * ur - ci * ui - wr)
            ri = object_weight * (cr * ui + ci * ur - wi)
            vr = -(cr * rr + ci * ri)
            vi = ci * rr - cr * ri
            if z == 0:
                vr = vr + data_weight * (data[0, 0] - ur)
                vi = vi + data_weight * (data[0, 1] - ui)
            values.append((vr, vi))
            resid.append((rr, ri))
        stage_one(values, k1, depth, -1, keep)
        stage_one(resid, k1, depth, -1, keep_resid)
    finish(spec, depth, rest, keep, 0)
    finish(spec, depth, rest, keep_resid, 1)


def descent_kernel(*refs):
    *fields, descent, sums, keep_in = refs
    depth = descent.shape[1]
    width, rest = factors(depth)
    invert_one(fields, depth, width, rest, keep_in)
    total = jnp.zeros(sums.shape[3:], F32)
    for k1 in range(width):
        for k0, (dr, di) in enumerate(stage_two(k1, width, depth, 1, keep_in)):
            put(descent, k1 + width * k0, (dr, di))
            total = total + (dr * dr + di * di)
    sums[0, 0, 0] = total


def image_kernel(descent, chi, *refs):
    *fields, image, sums, keep_in = refs
    depth = descent.shape[1]
    width, rest = factors(depth)
    invert_one(fields, depth, width, rest, keep_in)
    change = plane = jnp.zeros(sums.shape[3:], F32)
    for k1 in range(width):
        for k0, (hr, hi) in enumerate(stage_two(k1, width, depth, 1, keep_in)):
            z = k1 + width * k0
            put(image, z, (hr, hi))
            dr, di = pair(descent, z)
            cr, ci = chi[0, z], chi[1, z]
            qr = dr - (cr * hr - ci * hi)
            qi = di - (cr * hi + ci * hr)
            change = change + (qr * qr + qi * qi)
            if z == 0:
                plane = hr * hr + hi * hi
    sums[0, 0, 0] = change
    sums[0, 0, 1] = plane


def step_kernel(last, scal, source, descent, field, image, source_out, *rest_refs):
    if last:
        (parts,) = rest_refs
    else:
        field_out, parts = rest_refs
    sources, depth = source.shape[:2]
    step = scal[0, 0]

    def body(z, _):
        nr = ni = power = None
        for s in range(sources):
            dr, di = descent[s, z, 0], descent[s, z, 1]
            wr, wi = source[s, z, 0] + step * dr, source[s, z, 1] + step * di
            source_out[s, z, 0] = wr
            source_out[s, z, 1] = wi
            ur = field[s, z, 0] + step * image[s, z, 0]
            ui = field[s, z, 1] + step * image[s, z, 1]
            if not last:
                field_out[s, z, 0] = ur
                field_out[s, z, 1] = ui
            a, b, c = wr * ur + wi * ui, wi * ur - wr * ui, ur * ur + ui * ui
            nr, ni, power = (a, b, c) if s == 0 else (nr + a, ni + b, power + c)
        parts[0, z] = nr
        parts[1, z] = ni
        parts[2, z] = power
        return 0

    lax.fori_loop(0, depth, body, 0, unroll=4)


def assemble_kernel(spot, *refs):
    *rounds, out = refs
    turn = lax.rem(spot[0] + len(rounds) - pl.program_id(0), len(rounds))
    for t, ref in enumerate(rounds):

        @pl.when(turn == t)
        def _(ref=ref):
            for z in range(out.shape[2]):
                out[:, 0, z] = ref[:, z, 0]
                out[:, 1, z] = ref[:, z, 1]


def half_tables(total, order):
    half = total // 2
    modes = np.arange(half)[:, None]
    place = np.asarray(order)[None, :]
    out = []
    for odd in (0, 1):
        angle = 2.0 * math.pi * ((2 * modes + odd) * place % total) / total
        cosine, sine = np.cos(angle), np.sin(angle)
        out.append(np.block([[cosine, sine], [-sine, cosine]]).astype(np.float32))
    return np.stack(out)


def high_low(table):
    high = table.astype(ml_dtypes.bfloat16)
    low = (table - high.astype(np.float32)).astype(ml_dtypes.bfloat16)
    return np.stack([high, low])


def lateral_modes(total):
    index = np.concatenate([np.arange(0, total, 2), np.arange(1, total, 2)])
    return (4.0 * np.sin(math.pi * index / total) ** 2).astype(np.float32)


def split(value):
    high = value.astype(jnp.bfloat16)
    return high, (value - high.astype(F32)).astype(jnp.bfloat16)


def left_mul(table, odd, value):
    high, low = split(value)
    return jnp.dot(
        jnp.concatenate([table[0, odd], table[0, odd], table[1, odd]], axis=1),
        jnp.concatenate([high, low, high], axis=0),
        preferred_element_type=F32,
    )


def right_mul(value, table, odd):
    high, low = split(value)
    return jnp.dot(
        jnp.concatenate([high, low, high], axis=1),
        jnp.concatenate([table[0, odd], table[0, odd], table[1, odd]], axis=0),
        preferred_element_type=F32,
    )


def lateral(items, xf, yf):
    hx, ny = items[0][0][0].shape
    hy = ny // 2
    joined = lambda pick: jnp.concatenate(
        [jnp.concatenate([pick(own[c], other[c]) for c in (0, 1)], axis=0) for own, other in items], axis=1
    )
    across = [left_mul(xf, 0, joined(lambda a, b: a + b)), left_mul(xf, 1, joined(lambda a, b: a - b))]
    spectra = [[], []]
    for odd in (0, 1):
        folded = []
        for i in range(len(items)):
            low, high = i * ny, i * ny + hy
            parts = []
            for c in (0, 1):
                rows = slice(c * hx, (c + 1) * hx)
                left = jnp.concatenate([across[p][rows, low : low + hy] for p in (0, 1)], axis=0)
                right = jnp.concatenate([across[p][rows, high : high + hy] for p in (0, 1)], axis=0)
                parts.append(left - right if odd else left + right)
            folded.append(jnp.concatenate(parts, axis=1))
        freq = right_mul(jnp.concatenate(folded, axis=0), yf, odd)
        for i in range(len(items)):
            piece = freq[i * 2 * hx : (i + 1) * 2 * hx]
            spectra[odd].append((piece[:, :hy], piece[:, hy:]))
    return spectra


def lateral_back(spectra, xb, yb, out):
    senders, count, _, _, rows, ny = out.shape
    hx, hy = senders * rows, ny // 2
    back = [
        right_mul(jnp.concatenate([jnp.concatenate(v, axis=1) for v in spectra[odd]], axis=0), yb, odd)
        for odd in (0, 1)
    ]
    plus, minus = back[0] + back[1], back[0] - back[1]

    def joined(p):
        items = []
        for i in range(count):
            rows = slice((2 * i + p) * hx, (2 * i + p + 1) * hx)
            real = jnp.concatenate([plus[rows, :hy], minus[rows, :hy]], axis=1)
            imag = jnp.concatenate([plus[rows, hy:], minus[rows, hy:]], axis=1)
            items.append(jnp.concatenate([real, imag], axis=0))
        return jnp.concatenate(items, axis=1)

    even, odd = left_mul(xb, 0, joined(0)), left_mul(xb, 1, joined(1))
    plus, minus = even + odd, even - odd
    for i in range(count):
        for c in (0, 1):
            place = (slice(c * hx, (c + 1) * hx), slice(i * ny, (i + 1) * ny))
            out[:, i, c, 0] = plus[place].reshape(senders, rows, ny)
            out[:, i, c, 1] = minus[place].reshape(senders, rows, ny)


def filtered(values, sign, scale, lz, lx, ly, odd):
    wave_sq = WAVENUMBER * WAVENUMBER
    out = []
    for i, (fr, fi) in enumerate(values):
        eigen = (lx[...] + lz[pl.program_id(0) * len(values) + i]) + ly[odd]
        real_den = eigen - wave_sq
        imag_den = wave_sq * DAMPING
        factor = (wave_sq * scale) / (real_den * real_den + imag_den * imag_den)
        gr, gi = factor * real_den, factor * (imag_den * sign)
        out.append((fr * gr - fi * gi, fr * gi + fi * gr))
    return out


def loaded(own, other, *at):
    plane = lambda ref, i: [ref[(slice(None), i, *at, c)].reshape(-1, ref.shape[-1]) for c in (0, 1)]
    return [(plane(own, i), plane(other, i)) for i in range(own.shape[1])]


def plane_kernel(scale, lz, lx, ly, xf, xb, yf, yb, own, other, out):
    spectra = lateral(loaded(own, other), xf, yf)
    lateral_back([filtered(spectra[odd], 1.0, scale, lz, lx, ly, odd) for odd in (0, 1)], xb, yb, out)


def adjoint_plane_kernel(scale, lz, lx, ly, xf, xb, yf, yb, own, other, out, keep):
    inner = lateral(loaded(own, other, 0), xf, yf)
    resid = lateral(loaded(own, other, 1), xf, yf)
    spectra = []
    for odd in (0, 1):
        values = []
        for i, (re, im) in enumerate(filtered(inner[odd], -1.0, scale, lz, lx, ly, odd)):
            re, im = re + scale * resid[odd][i][0], im + scale * resid[odd][i][1]
            keep[i, odd, 0], keep[i, odd, 1] = re, im
            values.append((re, im))
        spectra.append(values)
    lateral_back(spectra, xb, yb, out)


def image_plane_kernel(lz, lx, ly, xb, yb, kept, out):
    spectra = [
        filtered([(kept[i, odd, 0], kept[i, odd, 1]) for i in range(kept.shape[0])], 1.0, 1.0, lz, lx, ly, odd)
        for odd in (0, 1)
    ]
    lateral_back(spectra, xb, yb, out)


SMEM = pl.BlockSpec(memory_space=pltpu.SMEM)


class Slabs:
    def __init__(self, sources, depth, rows, ny, pieces):
        self.sources, self.depth, self.rows, self.ny, self.pieces = sources, depth, rows, ny, pieces
        self.lanes = 128 if ny % 128 == 0 else ny
        self.deep = depth // 4 if depth % 4 == 0 else depth

    def kind(self, name, chunk):
        s, z, q, y, lanes, deep = self.sources, self.depth, self.rows, self.ny, self.lanes, self.deep
        turns = (y // lanes, s)
        if name.startswith("piece"):
            count = self.pieces[int(name[5:])]
            owners = z // sum(self.pieces)
            return (
                (s * owners, count, 2, 2, q, y),
                (owners, count, 2, 1, q, lanes),
                lambda j, i: (i, 0, 0, chunk, 0, j),
            )
        return {
            "field": ((s, z, 2, q, y), (1, z, 2, q, lanes), lambda j, i: (i, 0, 0, 0, j)),
            "spec": ((s * z, 2, q, y), (z, 2, q, lanes), lambda j, i: (i, 0, 0, j)),
            "twin": ((s * z, 2, 2, q, y), (z, 2, 2, q, lanes), lambda j, i: (i, 0, 0, 0, j)),
            "chi": ((2, z, q, y), (2, z, q, lanes), lambda j, i: (0, 0, 0, j)),
            "data": ((s, 2, q, y), (1, 2, q, lanes), lambda j, i: (i, 0, 0, j)),
            "sum1": (turns + (1, q, lanes), (1, 1, 1, q, lanes), lambda j, i: (j, i, 0, 0, 0)),
            "sum2": (turns + (2, q, lanes), (1, 1, 2, q, lanes), lambda j, i: (j, i, 0, 0, 0)),
            "every": ((s, z, 2, q, y), (s, deep, 2, q, lanes), lambda j, i: (0, i, 0, 0, j)),
            "parts": ((3, z, q, y), (3, deep, q, lanes), lambda j, i: (0, i, 0, j)),
        }[name]

    def call(self, kernel, chunk, ins, outs, scratch, *args):
        def spec(kind):
            if kind == "scal":
                return SMEM
            _, block, index = self.kind(kind, chunk)
            return pl.BlockSpec(block, index)

        sizes = [math.prod(self.kind(k, chunk)[0]) * 4 for k in (*ins, *outs) if k != "scal"]
        moved = sum(sizes)
        second = self.depth // self.deep if "parts" in outs else self.sources
        return pl.pallas_call(
            kernel,
            grid=(self.ny // self.lanes, second),
            in_specs=[spec(k) for k in ins],
            out_specs=[spec(k) for k in outs],
            out_shape=[jax.ShapeDtypeStruct(self.kind(k, chunk)[0], F32) for k in outs],
            scratch_shapes=[pltpu.VMEM((self.depth, 2, self.rows, self.lanes), F32)] * scratch,
            cost_estimate=pl.CostEstimate(flops=moved * 4, bytes_accessed=moved, transcendentals=0),
        )(*args)

    def piece_kinds(self):
        return tuple("piece%d" % m for m in range(len(self.pieces)))


def plane_call(kernel, senders, lz, tables, ins, work, rows, ny, kept_in=None, keeps=False):
    planes = lz.shape[0]
    group = 2 if planes % 2 == 0 else 1
    dense = rows % 8 != 0
    lead, deep = (1, senders * rows) if dense else (senders, rows)

    def shaped(value):
        inner = value.shape[1:-2]
        value = value.reshape((senders, planes) + value.shape[1:])
        if dense:
            value = jnp.moveaxis(value, 0, -3).reshape((1, planes) + inner + (deep, ny))
        return value

    ins = [shaped(v) for v in ins]
    nx = 2 * senders * rows
    whole = lambda t: pl.BlockSpec(t.shape, lambda i, n=t.ndim: (0,) * n)
    plane = lambda shape: pl.BlockSpec(
        (shape[0], group) + tuple(shape[2:]), lambda i, n=len(shape): (0, i) + (0,) * (n - 2)
    )
    kept = (planes, 2, 2, nx, ny // 2)
    kept_spec = pl.BlockSpec((group,) + kept[1:], lambda i: (i, 0, 0, 0, 0))
    out_shape = (lead, planes, 2, 2, deep, ny)
    shapes, specs = [jax.ShapeDtypeStruct(out_shape, F32)], [plane(out_shape)]
    if keeps:
        shapes.append(jax.ShapeDtypeStruct(kept, F32))
        specs.append(kept_spec)
    result = pl.pallas_call(
        kernel,
        grid=(planes // group,),
        in_specs=[SMEM] + [whole(t) for t in tables] + [plane(v.shape) for v in ins]
        + ([kept_spec] if kept_in is not None else []),
        out_specs=specs,
        out_shape=shapes,
        cost_estimate=pl.CostEstimate(
            flops=planes * work * 3 * nx * nx * ny * 2,
            bytes_accessed=work * math.prod(out_shape),
            transcendentals=0,
        ),
    )(lz, *tables, *ins, *([kept_in] if kept_in is not None else []))
    out = result[0]
    if dense:
        out = jnp.moveaxis(out.reshape((planes, 2, 2, senders, rows, ny)), 3, 0)
    return (out, result[1]) if keeps else out


def everyone(values):
    count = math.prod(lax.axis_size(name) for name in ALL)
    row = jnp.zeros((128,), F32).at[: len(values)].set(jnp.stack(values))
    sent = jnp.broadcast_to(row[None], (count, 128))
    return jnp.sum(lax.all_to_all(sent, ALL, 0, 0, tiled=True), axis=0)


def swap_halves(value):
    return lax.ppermute(value, "half", [(0, 1), (1, 0)])


def after(value, *others):
    return lax.optimization_barrier((value, *others))[0]


def bounded(numer_real, numer_imag, power, total_sources):
    floored = jnp.maximum(power, FLOOR_SHARE * total_sources)
    return jnp.stack(
        [
            jnp.clip(numer_real / floored, REAL_LOW, REAL_HIGH),
            jnp.clip(numer_imag / floored, 0.0, IMAG_HIGH),
        ]
    )


def payloads(chunks, shares, per_share, share):
    sent = []
    for t in range(shares):
        number = lax.rem(share + t, shares)
        cut = [lax.dynamic_slice_in_dim(w, number // 2 * per_share, per_share, axis=0) for w in chunks]
        sent.append(jnp.where(number % 2 == 0, cut[0], cut[1]))
    return sent


def deliver(sent, shares, per_share, share, half, gate):
    slots = shares // 2
    rounds = []
    for t in range(shares):
        pairs = []
        for a in range(shares):
            g, c = divmod((a + t) % shares, 2)
            for h in (0, 1):
                pairs.append((a * 2 + h, (h * slots + g) * 2 + (h + c) % 2))
        rounds.append(lax.ppermute(sent[t], ("src", "half"), pairs))
    spot = after(2 * lax.rem(share, slots) + lax.rem(half + share // slots, 2), gate)
    _, depth, _, rows, ny = rounds[0].shape
    whole = pl.BlockSpec(rounds[0].shape, lambda a: (0, 0, 0, 0, 0))
    out = pl.pallas_call(
        assemble_kernel,
        grid=(shares,),
        in_specs=[SMEM] + [whole] * shares,
        out_specs=pl.BlockSpec((per_share, 2, depth, None, rows, ny), lambda a: (0, 0, 0, a, 0, 0)),
        out_shape=jax.ShapeDtypeStruct((per_share, 2, depth, shares, rows, ny), F32),
        name="assemble",
    )(spot.reshape(1).astype(jnp.int32), *rounds)
    return out.reshape(per_share, 2, depth, shares * rows, ny)


def on_device(contrast, measured, positions):
    shares, rest_count = lax.axis_size("src"), lax.axis_size("rest")
    share, half, rest = (lax.axis_index(name) for name in ALL)
    senders = shares * rest_count
    _, depth, block_rows, ny = contrast.shape
    rows = block_rows // shares
    nx = block_rows * 2 * rest_count
    per_share = positions.shape[0]
    total_sources = per_share * shares
    sources = total_sources // 2
    planes = sources * depth // senders
    slabs = Slabs(sources, depth, rows, ny, (planes,))

    chi_own = lax.dynamic_index_in_dim(
        contrast.reshape(2, depth, shares, rows, ny), share, axis=2, keepdims=False
    )
    chi = [chi_own, swap_halves(chi_own)]

    spots = jnp.pad(positions.astype(F32).reshape(1, -1), ((0, 0), (0, 126)))
    sent = jnp.concatenate(
        [
            measured.reshape(per_share, 2, shares, rows * ny).transpose(2, 0, 1, 3).reshape(shares, -1),
            jnp.broadcast_to(spots, (shares, spots.shape[1])),
        ],
        axis=1,
    )
    got = lax.all_to_all(sent, "src", 0, 0, tiled=True)
    cells = per_share * 2 * rows * ny
    data_own = got[:, :cells].reshape(total_sources, 2, rows, ny)
    spots = got[:, cells : cells + 2 * per_share].reshape(total_sources, 2)
    mine = lambda v, h: lax.dynamic_slice_in_dim(v, h * sources, sources, axis=0)
    data = [mine(data_own, half), swap_halves(mine(data_own, 1 - half))]
    spots = mine(spots, half)

    heights = jnp.arange(depth).astype(F32) + SOURCE_GAP
    offset_y = jnp.arange(ny).astype(F32)[None] - spots[:, 1][:, None]
    inc = []
    for where in (half, 1 - half):
        start = (where * rest_count + rest) * block_rows + share * rows
        offset_x = (start + jnp.arange(rows)).astype(F32)[None] - spots[:, 0][:, None]
        dist_sq = (heights * heights)[None, :, None, None] + (offset_x * offset_x)[:, None, :, None]
        dist_sq = dist_sq + (offset_y * offset_y)[:, None, None, :]
        phases = WAVENUMBER * jnp.sqrt(dist_sq)
        inc.append(jnp.stack([jnp.cos(phases), jnp.sin(phases)], axis=2))

    order = [(k * shares + a) * rows + q for a in range(shares) for k in range(rest_count) for q in range(rows)]
    x_table, y_table = half_tables(nx, order), half_tables(ny, range(ny // 2))
    flip = lambda t: high_low(np.swapaxes(t, -1, -2))
    lx = np.broadcast_to(lateral_modes(nx)[:, None], (nx, ny // 2))
    ly = lateral_modes(ny).reshape(2, 1, ny // 2)
    lx, ly, xf, xb, yf, yb = (
        jnp.asarray(t) for t in (lx, ly, high_low(x_table), flip(x_table), flip(y_table), high_low(y_table))
    )
    place = share * rest_count + rest
    modes = (place * planes + jnp.arange(planes)) % depth
    half_sine = jnp.sin(math.pi * modes.astype(F32) / depth)
    lz = 4.0 * half_sine * half_sine
    scale = 1.0 / (nx * ny * depth)

    def exchange(value):
        flat = value.reshape((senders * planes,) + value.shape[-4:])
        return lax.all_to_all(flat, GROUP, 0, 0, tiled=True).reshape(value.shape)

    call_planes = lambda kernel, tables, ins, work, **kw: plane_call(
        kernel, senders, lz, tables, ins, work, rows, ny, **kw
    )
    tables = (lx, ly, xf, xb, yf, yb)

    both = (0, 1)
    piece_kinds = slabs.piece_kinds()
    totals = everyone([jnp.sum(measured * measured), total_sources * jnp.sum(chi_own * chi_own)])
    data_weight = 1.0 / totals[0]
    object_total = totals[1]
    source, came = [None, None], [None, None]
    for c in both:
        source[c], spec = slabs.call(start_kernel, c, ("chi", "field"), ("field", "spec"), 1, chi[c], inc[c])
        came[c] = lax.all_to_all(spec, GROUP, 0, 0, tiled=True)
    fields = exchange(call_planes(partial(plane_kernel, scale), tables, came, 8))
    total = [None, None]
    for outer in range(OUTER):
        object_weight = 1.0 / object_total
        weights = jnp.stack([object_weight, data_weight]).reshape(1, 2)
        first, last = outer == 0, outer == OUTER - 1
        descent, image, came = [None, None], [None, None], [None, None]
        for c in both:
            out = slabs.call(
                partial(adjoint_kernel, first),
                c,
                ("scal", "chi", "field", "data", "field") + (piece_kinds if first else ()),
                ("field", "twin") if first else ("twin",),
                3 if first else 2,
                weights, chi[c], source[c], data[c] + inc[c][:, 0],
                *((inc[c], fields) if first else (total[c],)),
            )
            if first:
                total[c] = out[0]
            came[c] = lax.all_to_all(out[-1], GROUP, 0, 0, tiled=True)
        part, kept = call_planes(partial(adjoint_plane_kernel, scale), tables, came, 12, keeps=True)
        fields = exchange(part)
        fields_image = exchange(call_planes(image_plane_kernel, (lx, ly, xb, yb), [], 4, kept_in=kept))
        sums = []
        for c in both:
            descent[c], part = slabs.call(descent_kernel, c, piece_kinds, ("field", "sum1"), 1, fields)
            sums.append(part)
        sum_d = jnp.sum(sums[0]) + jnp.sum(sums[1])
        sums = []
        for c in both:
            image[c], part = slabs.call(
                image_kernel, c, ("field", "chi") + piece_kinds, ("field", "sum2"), 1,
                descent[c], chi[c], fields_image,
            )
            sums.append(part)
        sum_q = sums[0] + sums[1]
        totals = everyone([sum_d, jnp.sum(sum_q[:, :, 0]), jnp.sum(sum_q[:, :, 1])])
        step = totals[0] / (data_weight * totals[2] + object_weight * totals[1])
        parts = [None, None]
        for c in (1, 0):
            out = slabs.call(
                partial(step_kernel, last),
                c,
                ("scal",) + ("every",) * 4,
                ("every",) * (1 if last else 2) + ("parts",),
                0,
                step.reshape(1, 1), source[c], descent[c], total[c], image[c],
            )
            source[c], parts[c] = out[0], out[-1]
            if not last:
                total[c] = out[1]
        received = swap_halves(parts[1])
        if last:
            sent = payloads(source, shares, per_share, share)
            received, *sent = lax.optimization_barrier((received, *sent))
        sums = parts[0] + received
        chi_own = bounded(sums[0], sums[1], sums[2], total_sources)
        if not last:
            object_total = everyone([total_sources * jnp.sum(chi_own * chi_own)])[0]
            chi = [chi_own, swap_halves(after(chi_own, object_total))]

    copies = jnp.broadcast_to(chi_own[None], (shares,) + chi_own.shape)
    contrast_new = lax.all_to_all(copies, "src", 0, 0, tiled=True)
    contrast_new = contrast_new.transpose(1, 2, 0, 3, 4).reshape(contrast.shape)
    contrast_sources = deliver(sent, shares, per_share, share, half, contrast_new)
    return contrast_sources, contrast_new


def solution(mesh):
    shares, spaces = mesh.shape["src"], mesh.shape["space"]
    split_mesh = Mesh(mesh.devices.reshape(shares, 2, spaces // 2), ALL)
    space = ("half", "rest")

    return jax.shard_map(
        on_device,
        mesh=split_mesh,
        in_specs=(P(None, None, space, None), P("src", None, space, None), P("src", None)),
        out_specs=(P("src", None, None, space, None), P(None, None, space, None)),
        check_vma=False,
    )
```

```python
from functools import partial
import math

import jax
import jax.numpy as jnp
import ml_dtypes
import numpy as np
from jax import lax
from jax.experimental import pallas as pl
from jax.experimental.pallas import tpu as pltpu
from jax.sharding import Mesh, PartitionSpec as P


OUTER = 2
WAVENUMBER = 2.0 * math.pi / 6.0
DAMPING = 0.3
SOURCE_GAP = 8.0
FLOOR_SHARE = 0.75
REAL_LOW = -0.25
REAL_HIGH = 0.35
IMAG_HIGH = 0.1
ALL = ("src", "half", "rest")
GROUP = ("src", "rest")
F32 = jnp.float32


def times_const(value, factor):
    re, im = value
    a, b = factor.real, factor.imag
    if abs(b) < 1e-12:
        return (re, im) if abs(a - 1) < 1e-12 else (re * a, im * a)
    if abs(a) < 1e-12:
        return (im * -b, re * b) if abs(abs(b) - 1) > 1e-12 else ((-im, re) if b > 0 else (im, -re))
    if abs(abs(a) - abs(b)) < 1e-12:
        if a * b > 0:
            return ((re - im) * a, (re + im) * a)
        return ((re + im) * a, (im - re) * a)
    return (re * a - im * b, re * b + im * a)


def small_dft(values, sign):
    count = len(values)
    if count == 1:
        return values
    even, odd = small_dft(values[0::2], sign), small_dft(values[1::2], sign)
    low, high = [], []
    for k in range(count // 2):
        turned = times_const(odd[k], np.exp(sign * 2j * math.pi * k / count))
        low.append((even[k][0] + turned[0], even[k][1] + turned[1]))
        high.append((even[k][0] - turned[0], even[k][1] - turned[1]))
    return low + high


def factors(total):
    bits = total.bit_length() - 1
    return 1 << (bits // 2), total // (1 << (bits // 2))


def stage_one(values, n0, count, sign, keep):
    width = len(values)
    for k1, value in enumerate(small_dft(values, sign)):
        re, im = times_const(value, np.exp(sign * 2j * math.pi * n0 * k1 / count))
        keep[n0 * width + k1, 0] = re
        keep[n0 * width + k1, 1] = im


def stage_two(k1, width, count, sign, keep):
    values = [(keep[n0 * width + k1, 0], keep[n0 * width + k1, 1]) for n0 in range(count // width)]
    return small_dft(values, sign)


def pair(ref, z):
    return ref[0, z, 0], ref[0, z, 1]


def put(ref, z, value):
    ref[0, z, 0] = value[0]
    ref[0, z, 1] = value[1]


def returned(refs, z):
    place, plane = divmod(z, sum(ref.shape[1] for ref in refs))
    for ref in refs:
        if plane < ref.shape[1]:
            return ref[place, plane, 0, 0], ref[place, plane, 1, 0]
        plane -= ref.shape[1]


def invert_one(refs, depth, width, rest, keep):
    for n0 in range(rest):
        stage_one([returned(refs, n0 + rest * n1) for n1 in range(width)], n0, depth, 1, keep)


def finish(spec, depth, rest, keep, *at):
    for j1 in range(rest):
        for j0, (re, im) in enumerate(stage_two(j1, rest, depth, -1, keep)):
            spec[(j1 + rest * j0, *at, 0)] = re
            spec[(j1 + rest * j0, *at, 1)] = im


def start_kernel(chi, inc, source, spec, keep):
    depth = inc.shape[1]
    width, rest = factors(depth)
    for n0 in range(width):
        values = []
        for n1 in range(rest):
            z = n0 + width * n1
            cr, ci = chi[0, z], chi[1, z]
            er, ei = pair(inc, z)
            w = (cr * er - ci * ei, cr * ei + ci * er)
            put(source, z, w)
            values.append(w)
        stage_one(values, n0, depth, -1, keep)
    finish(spec, depth, rest, keep)


def adjoint_kernel(first, scal, chi, source, data, field, *refs):
    if first:
        *fields, total_out, spec, keep_in, keep, keep_resid = refs
    else:
        spec, keep, keep_resid = refs
    depth = source.shape[1]
    width, rest = factors(depth)
    object_weight, data_weight = scal[0, 0], scal[0, 1]
    if first:
        invert_one(fields, depth, width, rest, keep_in)
    for k1 in range(width):
        scattered = stage_two(k1, width, depth, 1, keep_in) if first else None
        values, resid = [], []
        for k0 in range(rest):
            z = k1 + width * k0
            ur, ui = pair(field, z)
            if first:
                ur, ui = ur + scattered[k0][0], ui + scattered[k0][1]
                put(total_out, z, (ur, ui))
            cr, ci = chi[0, z], chi[1, z]
            wr, wi = pair(source, z)
            rr = object_weight * (cr * ur - ci * ui - wr)
            ri = object_weight * (cr * ui + ci * ur - wi)
            vr = -(cr * rr + ci * ri)
            vi = ci * rr - cr * ri
            if z == 0:
                vr = vr + data_weight * (data[0, 0] - ur)
                vi = vi + data_weight * (data[0, 1] - ui)
            values.append((vr, vi))
            resid.append((rr, ri))
        stage_one(values, k1, depth, -1, keep)
        stage_one(resid, k1, depth, -1, keep_resid)
    finish(spec, depth, rest, keep, 0)
    finish(spec, depth, rest, keep_resid, 1)


def descent_kernel(*refs):
    *fields, descent, sums, keep_in = refs
    depth = descent.shape[1]
    width, rest = factors(depth)
    invert_one(fields, depth, width, rest, keep_in)
    total = jnp.zeros(sums.shape[3:], F32)
    for k1 in range(width):
        for k0, (dr, di) in enumerate(stage_two(k1, width, depth, 1, keep_in)):
            put(descent, k1 + width * k0, (dr, di))
            total = total + (dr * dr + di * di)
    sums[0, 0, 0] = total


def image_kernel(descent, chi, *refs):
    *fields, image, sums, keep_in = refs
    depth = descent.shape[1]
    width, rest = factors(depth)
    invert_one(fields, depth, width, rest, keep_in)
    change = plane = jnp.zeros(sums.shape[3:], F32)
    for k1 in range(width):
        for k0, (hr, hi) in enumerate(stage_two(k1, width, depth, 1, keep_in)):
            z = k1 + width * k0
            put(image, z, (hr, hi))
            dr, di = pair(descent, z)
            cr, ci = chi[0, z], chi[1, z]
            qr = dr - (cr * hr - ci * hi)
            qi = di - (cr * hi + ci * hr)
            change = change + (qr * qr + qi * qi)
            if z == 0:
                plane = hr * hr + hi * hi
    sums[0, 0, 0] = change
    sums[0, 0, 1] = plane


def step_kernel(last, scal, source, descent, field, image, source_out, *rest_refs):
    if last:
        (parts,) = rest_refs
    else:
        field_out, parts = rest_refs
    sources, depth = source.shape[:2]
    step = scal[0, 0]

    def body(z, _):
        nr = ni = power = None
        for s in range(sources):
            dr, di = descent[s, z, 0], descent[s, z, 1]
            wr, wi = source[s, z, 0] + step * dr, source[s, z, 1] + step * di
            source_out[s, z, 0] = wr
            source_out[s, z, 1] = wi
            ur = field[s, z, 0] + step * image[s, z, 0]
            ui = field[s, z, 1] + step * image[s, z, 1]
            if not last:
                field_out[s, z, 0] = ur
                field_out[s, z, 1] = ui
            a, b, c = wr * ur + wi * ui, wi * ur - wr * ui, ur * ur + ui * ui
            nr, ni, power = (a, b, c) if s == 0 else (nr + a, ni + b, power + c)
        parts[0, z] = nr
        parts[1, z] = ni
        parts[2, z] = power
        return 0

    lax.fori_loop(0, depth, body, 0, unroll=4)


def assemble_kernel(shares, spot, *refs):
    *rounds, out = refs
    turn = spot[0] * shares + lax.rem(pl.program_id(0) + shares - spot[1], shares)
    for t, ref in enumerate(rounds):

        @pl.when(turn == t)
        def _(ref=ref):
            for z in range(out.shape[2]):
                out[:, 0, z] = ref[:, z, 0]
                out[:, 1, z] = ref[:, z, 1]


def half_tables(total, order):
    half = total // 2
    modes = np.arange(half)[:, None]
    place = np.asarray(order)[None, :]
    out = []
    for odd in (0, 1):
        angle = 2.0 * math.pi * ((2 * modes + odd) * place % total) / total
        cosine, sine = np.cos(angle), np.sin(angle)
        out.append(np.block([[cosine, sine], [-sine, cosine]]).astype(np.float32))
    return np.stack(out)


def high_low(table):
    high = table.astype(ml_dtypes.bfloat16)
    low = (table - high.astype(np.float32)).astype(ml_dtypes.bfloat16)
    return np.stack([high, low])


def lateral_modes(total):
    index = np.concatenate([np.arange(0, total, 2), np.arange(1, total, 2)])
    return (4.0 * np.sin(math.pi * index / total) ** 2).astype(np.float32)


def split(value):
    high = value.astype(jnp.bfloat16)
    return high, (value - high.astype(F32)).astype(jnp.bfloat16)


def left_mul(table, odd, value):
    high, low = split(value)
    return jnp.dot(
        jnp.concatenate([table[0, odd], table[0, odd], table[1, odd]], axis=1),
        jnp.concatenate([high, low, high], axis=0),
        preferred_element_type=F32,
    )


def right_mul(value, table, odd):
    high, low = split(value)
    return jnp.dot(
        jnp.concatenate([high, low, high], axis=1),
        jnp.concatenate([table[0, odd], table[0, odd], table[1, odd]], axis=0),
        preferred_element_type=F32,
    )


def lateral(items, xf, yf):
    hx, ny = items[0][0][0].shape
    hy = ny // 2
    joined = lambda pick: jnp.concatenate(
        [jnp.concatenate([pick(own[c], other[c]) for c in (0, 1)], axis=0) for own, other in items], axis=1
    )
    across = [left_mul(xf, 0, joined(lambda a, b: a + b)), left_mul(xf, 1, joined(lambda a, b: a - b))]
    spectra = [[], []]
    for odd in (0, 1):
        folded = []
        for i in range(len(items)):
            low, high = i * ny, i * ny + hy
            parts = []
            for c in (0, 1):
                rows = slice(c * hx, (c + 1) * hx)
                left = jnp.concatenate([across[p][rows, low : low + hy] for p in (0, 1)], axis=0)
                right = jnp.concatenate([across[p][rows, high : high + hy] for p in (0, 1)], axis=0)
                parts.append(left - right if odd else left + right)
            folded.append(jnp.concatenate(parts, axis=1))
        freq = right_mul(jnp.concatenate(folded, axis=0), yf, odd)
        for i in range(len(items)):
            piece = freq[i * 2 * hx : (i + 1) * 2 * hx]
            spectra[odd].append((piece[:, :hy], piece[:, hy:]))
    return spectra


def lateral_back(spectra, xb, yb, out):
    senders, count, _, _, rows, ny = out.shape
    hx, hy = senders * rows, ny // 2
    back = [
        right_mul(jnp.concatenate([jnp.concatenate(v, axis=1) for v in spectra[odd]], axis=0), yb, odd)
        for odd in (0, 1)
    ]
    plus, minus = back[0] + back[1], back[0] - back[1]

    def joined(p):
        items = []
        for i in range(count):
            rows = slice((2 * i + p) * hx, (2 * i + p + 1) * hx)
            real = jnp.concatenate([plus[rows, :hy], minus[rows, :hy]], axis=1)
            imag = jnp.concatenate([plus[rows, hy:], minus[rows, hy:]], axis=1)
            items.append(jnp.concatenate([real, imag], axis=0))
        return jnp.concatenate(items, axis=1)

    even, odd = left_mul(xb, 0, joined(0)), left_mul(xb, 1, joined(1))
    plus, minus = even + odd, even - odd
    for i in range(count):
        for c in (0, 1):
            place = (slice(c * hx, (c + 1) * hx), slice(i * ny, (i + 1) * ny))
            out[:, i, c, 0] = plus[place].reshape(senders, rows, ny)
            out[:, i, c, 1] = minus[place].reshape(senders, rows, ny)


def filtered(values, sign, scale, lz, lx, ly, odd):
    wave_sq = WAVENUMBER * WAVENUMBER
    out = []
    for i, (fr, fi) in enumerate(values):
        eigen = (lx[...] + lz[pl.program_id(0) * len(values) + i]) + ly[odd]
        real_den = eigen - wave_sq
        imag_den = wave_sq * DAMPING
        factor = (wave_sq * scale) / (real_den * real_den + imag_den * imag_den)
        gr, gi = factor * real_den, factor * (imag_den * sign)
        out.append((fr * gr - fi * gi, fr * gi + fi * gr))
    return out


def loaded(own, other, *at):
    plane = lambda ref, i: [ref[(slice(None), i, *at, c)].reshape(-1, ref.shape[-1]) for c in (0, 1)]
    return [(plane(own, i), plane(other, i)) for i in range(own.shape[1])]


def plane_kernel(scale, lz, lx, ly, xf, xb, yf, yb, own, other, out):
    spectra = lateral(loaded(own, other), xf, yf)
    lateral_back([filtered(spectra[odd], 1.0, scale, lz, lx, ly, odd) for odd in (0, 1)], xb, yb, out)


def adjoint_plane_kernel(scale, lz, lx, ly, xf, xb, yf, yb, own, other, out, keep):
    inner = lateral(loaded(own, other, 0), xf, yf)
    resid = lateral(loaded(own, other, 1), xf, yf)
    spectra = []
    for odd in (0, 1):
        values = []
        for i, (re, im) in enumerate(filtered(inner[odd], -1.0, scale, lz, lx, ly, odd)):
            re, im = re + scale * resid[odd][i][0], im + scale * resid[odd][i][1]
            keep[i, odd, 0], keep[i, odd, 1] = re, im
            values.append((re, im))
        spectra.append(values)
    lateral_back(spectra, xb, yb, out)


def image_plane_kernel(lz, lx, ly, xb, yb, kept, out):
    spectra = [
        filtered([(kept[i, odd, 0], kept[i, odd, 1]) for i in range(kept.shape[0])], 1.0, 1.0, lz, lx, ly, odd)
        for odd in (0, 1)
    ]
    lateral_back(spectra, xb, yb, out)


SMEM = pl.BlockSpec(memory_space=pltpu.SMEM)


class Slabs:
    def __init__(self, sources, depth, rows, ny, pieces):
        self.sources, self.depth, self.rows, self.ny, self.pieces = sources, depth, rows, ny, pieces
        self.lanes = 128 if ny % 128 == 0 else ny
        self.deep = depth // 4 if depth % 4 == 0 else depth

    def kind(self, name, chunk):
        s, z, q, y, lanes, deep = self.sources, self.depth, self.rows, self.ny, self.lanes, self.deep
        turns = (y // lanes, s)
        if name.startswith("piece"):
            count = self.pieces[int(name[5:])]
            owners = z // sum(self.pieces)
            return (
                (s * owners, count, 2, 2, q, y),
                (owners, count, 2, 1, q, lanes),
                lambda j, i: (i, 0, 0, chunk, 0, j),
            )
        return {
            "field": ((s, z, 2, q, y), (1, z, 2, q, lanes), lambda j, i: (i, 0, 0, 0, j)),
            "spec": ((s * z, 2, q, y), (z, 2, q, lanes), lambda j, i: (i, 0, 0, j)),
            "twin": ((s * z, 2, 2, q, y), (z, 2, 2, q, lanes), lambda j, i: (i, 0, 0, 0, j)),
            "chi": ((2, z, q, y), (2, z, q, lanes), lambda j, i: (0, 0, 0, j)),
            "data": ((s, 2, q, y), (1, 2, q, lanes), lambda j, i: (i, 0, 0, j)),
            "sum1": (turns + (1, q, lanes), (1, 1, 1, q, lanes), lambda j, i: (j, i, 0, 0, 0)),
            "sum2": (turns + (2, q, lanes), (1, 1, 2, q, lanes), lambda j, i: (j, i, 0, 0, 0)),
            "every": ((s, z, 2, q, y), (s, deep, 2, q, lanes), lambda j, i: (0, i, 0, 0, j)),
            "parts": ((3, z, q, y), (3, deep, q, lanes), lambda j, i: (0, i, 0, j)),
        }[name]

    def call(self, kernel, chunk, ins, outs, scratch, *args):
        def spec(kind):
            if kind == "scal":
                return SMEM
            _, block, index = self.kind(kind, chunk)
            return pl.BlockSpec(block, index)

        sizes = [math.prod(self.kind(k, chunk)[0]) * 4 for k in (*ins, *outs) if k != "scal"]
        moved = sum(sizes)
        second = self.depth // self.deep if "parts" in outs else self.sources
        return pl.pallas_call(
            kernel,
            grid=(self.ny // self.lanes, second),
            in_specs=[spec(k) for k in ins],
            out_specs=[spec(k) for k in outs],
            out_shape=[jax.ShapeDtypeStruct(self.kind(k, chunk)[0], F32) for k in outs],
            scratch_shapes=[pltpu.VMEM((self.depth, 2, self.rows, self.lanes), F32)] * scratch,
            cost_estimate=pl.CostEstimate(flops=moved * 4, bytes_accessed=moved, transcendentals=0),
        )(*args)

    def piece_kinds(self):
        return tuple("piece%d" % m for m in range(len(self.pieces)))


def plane_call(kernel, senders, lz, tables, ins, work, rows, ny, kept_in=None, keeps=False):
    planes = lz.shape[0]
    group = 2 if planes % 2 == 0 else 1
    dense = rows % 8 != 0
    lead, deep = (1, senders * rows) if dense else (senders, rows)

    def shaped(value):
        inner = value.shape[1:-2]
        value = value.reshape((senders, planes) + value.shape[1:])
        if dense:
            value = jnp.moveaxis(value, 0, -3).reshape((1, planes) + inner + (deep, ny))
        return value

    ins = [shaped(v) for v in ins]
    nx = 2 * senders * rows
    whole = lambda t: pl.BlockSpec(t.shape, lambda i, n=t.ndim: (0,) * n)
    plane = lambda shape: pl.BlockSpec(
        (shape[0], group) + tuple(shape[2:]), lambda i, n=len(shape): (0, i) + (0,) * (n - 2)
    )
    kept = (planes, 2, 2, nx, ny // 2)
    kept_spec = pl.BlockSpec((group,) + kept[1:], lambda i: (i, 0, 0, 0, 0))
    out_shape = (lead, planes, 2, 2, deep, ny)
    shapes, specs = [jax.ShapeDtypeStruct(out_shape, F32)], [plane(out_shape)]
    if keeps:
        shapes.append(jax.ShapeDtypeStruct(kept, F32))
        specs.append(kept_spec)
    result = pl.pallas_call(
        kernel,
        grid=(planes // group,),
        in_specs=[SMEM] + [whole(t) for t in tables] + [plane(v.shape) for v in ins]
        + ([kept_spec] if kept_in is not None else []),
        out_specs=specs,
        out_shape=shapes,
        cost_estimate=pl.CostEstimate(
            flops=planes * work * 3 * nx * nx * ny * 2,
            bytes_accessed=work * math.prod(out_shape),
            transcendentals=0,
        ),
    )(lz, *tables, *ins, *([kept_in] if kept_in is not None else []))
    out = result[0]
    if dense:
        out = jnp.moveaxis(out.reshape((planes, 2, 2, senders, rows, ny)), 3, 0)
    return (out, result[1]) if keeps else out


def everyone(values):
    count = math.prod(lax.axis_size(name) for name in ALL)
    row = jnp.zeros((128,), F32).at[: len(values)].set(jnp.stack(values))
    sent = jnp.broadcast_to(row[None], (count, 128))
    return jnp.sum(lax.all_to_all(sent, ALL, 0, 0, tiled=True), axis=0)


def swap_halves(value):
    return lax.ppermute(value, "half", [(0, 1), (1, 0)])


def after(value, *others):
    return lax.optimization_barrier((value, *others))[0]


def bounded(numer_real, numer_imag, power, total_sources):
    floored = jnp.maximum(power, FLOOR_SHARE * total_sources)
    return jnp.stack(
        [
            jnp.clip(numer_real / floored, REAL_LOW, REAL_HIGH),
            jnp.clip(numer_imag / floored, 0.0, IMAG_HIGH),
        ]
    )


def payloads(chunks, shares, per_share, share):
    sent = []
    for w in chunks:
        for t in range(shares):
            slot = lax.rem(share + shares - t, shares) // 2
            sent.append(lax.dynamic_slice_in_dim(w, slot * per_share, per_share, axis=0))
    return sent


def deliver(sent, shares, chunk):
    slots = shares // 2
    rounds = []
    for t in range(shares):
        pairs = [
            ((t + 2 * g) % shares * 2 + h, (h * slots + g) * 2 + (h + chunk) % 2)
            for g in range(slots)
            for h in (0, 1)
        ]
        rounds.append(lax.ppermute(sent[t], ("src", "half"), pairs))
    return rounds


def assembled(rounds, shares, share, half, gate):
    slots = shares // 2
    chunk = lax.rem(share // slots + half, 2)
    spot = after(jnp.stack([chunk, 2 * lax.rem(share, slots)]).astype(jnp.int32), gate)
    per_share, depth, _, rows, ny = rounds[0].shape
    whole = pl.BlockSpec(rounds[0].shape, lambda a: (0, 0, 0, 0, 0))
    out = pl.pallas_call(
        partial(assemble_kernel, shares),
        grid=(shares,),
        in_specs=[SMEM] + [whole] * len(rounds),
        out_specs=pl.BlockSpec((per_share, 2, depth, None, rows, ny), lambda a: (0, 0, 0, a, 0, 0)),
        out_shape=jax.ShapeDtypeStruct((per_share, 2, depth, shares, rows, ny), F32),
        name="assemble",
    )(spot, *rounds)
    return out.reshape(per_share, 2, depth, shares * rows, ny)


def on_device(contrast, measured, positions):
    shares, rest_count = lax.axis_size("src"), lax.axis_size("rest")
    share, half, rest = (lax.axis_index(name) for name in ALL)
    senders = shares * rest_count
    _, depth, block_rows, ny = contrast.shape
    rows = block_rows // shares
    nx = block_rows * 2 * rest_count
    per_share = positions.shape[0]
    total_sources = per_share * shares
    sources = total_sources // 2
    planes = sources * depth // senders
    slabs = Slabs(sources, depth, rows, ny, (planes,))

    chi_own = lax.dynamic_index_in_dim(
        contrast.reshape(2, depth, shares, rows, ny), share, axis=2, keepdims=False
    )
    chi = [chi_own, swap_halves(chi_own)]

    spots = jnp.pad(positions.astype(F32).reshape(1, -1), ((0, 0), (0, 126)))
    sent = jnp.concatenate(
        [
            measured.reshape(per_share, 2, shares, rows * ny).transpose(2, 0, 1, 3).reshape(shares, -1),
            jnp.broadcast_to(spots, (shares, spots.shape[1])),
        ],
        axis=1,
    )
    got = lax.all_to_all(sent, "src", 0, 0, tiled=True)
    cells = per_share * 2 * rows * ny
    data_own = got[:, :cells].reshape(total_sources, 2, rows, ny)
    spots = got[:, cells : cells + 2 * per_share].reshape(total_sources, 2)
    mine = lambda v, h: lax.dynamic_slice_in_dim(v, h * sources, sources, axis=0)
    data = [mine(data_own, half), swap_halves(mine(data_own, 1 - half))]
    spots = mine(spots, half)

    heights = jnp.arange(depth).astype(F32) + SOURCE_GAP
    offset_y = jnp.arange(ny).astype(F32)[None] - spots[:, 1][:, None]
    inc = []
    for where in (half, 1 - half):
        start = (where * rest_count + rest) * block_rows + share * rows
        offset_x = (start + jnp.arange(rows)).astype(F32)[None] - spots[:, 0][:, None]
        dist_sq = (heights * heights)[None, :, None, None] + (offset_x * offset_x)[:, None, :, None]
        dist_sq = dist_sq + (offset_y * offset_y)[:, None, None, :]
        phases = WAVENUMBER * jnp.sqrt(dist_sq)
        inc.append(jnp.stack([jnp.cos(phases), jnp.sin(phases)], axis=2))

    order = [(k * shares + a) * rows + q for a in range(shares) for k in range(rest_count) for q in range(rows)]
    x_table, y_table = half_tables(nx, order), half_tables(ny, range(ny // 2))
    flip = lambda t: high_low(np.swapaxes(t, -1, -2))
    lx = np.broadcast_to(lateral_modes(nx)[:, None], (nx, ny // 2))
    ly = lateral_modes(ny).reshape(2, 1, ny // 2)
    lx, ly, xf, xb, yf, yb = (
        jnp.asarray(t) for t in (lx, ly, high_low(x_table), flip(x_table), flip(y_table), high_low(y_table))
    )
    place = share * rest_count + rest
    modes = (place * planes + jnp.arange(planes)) % depth
    half_sine = jnp.sin(math.pi * modes.astype(F32) / depth)
    lz = 4.0 * half_sine * half_sine
    scale = 1.0 / (nx * ny * depth)

    def exchange(value):
        flat = value.reshape((senders * planes,) + value.shape[-4:])
        return lax.all_to_all(flat, GROUP, 0, 0, tiled=True).reshape(value.shape)

    call_planes = lambda kernel, tables, ins, work, **kw: plane_call(
        kernel, senders, lz, tables, ins, work, rows, ny, **kw
    )
    tables = (lx, ly, xf, xb, yf, yb)

    both = (0, 1)
    piece_kinds = slabs.piece_kinds()
    totals = everyone([jnp.sum(measured * measured), total_sources * jnp.sum(chi_own * chi_own)])
    data_weight = 1.0 / totals[0]
    object_total = totals[1]
    source, came = [None, None], [None, None]
    for c in both:
        source[c], spec = slabs.call(start_kernel, c, ("chi", "field"), ("field", "spec"), 1, chi[c], inc[c])
        came[c] = lax.all_to_all(spec, GROUP, 0, 0, tiled=True)
    fields = exchange(call_planes(partial(plane_kernel, scale), tables, came, 8))
    total = [None, None]
    for outer in range(OUTER):
        object_weight = 1.0 / object_total
        weights = jnp.stack([object_weight, data_weight]).reshape(1, 2)
        first, last = outer == 0, outer == OUTER - 1
        descent, image, came = [None, None], [None, None], [None, None]
        for c in both:
            out = slabs.call(
                partial(adjoint_kernel, first),
                c,
                ("scal", "chi", "field", "data", "field") + (piece_kinds if first else ()),
                ("field", "twin") if first else ("twin",),
                3 if first else 2,
                weights, chi[c], source[c], data[c] + inc[c][:, 0],
                *((inc[c], fields) if first else (total[c],)),
            )
            if first:
                total[c] = out[0]
            came[c] = lax.all_to_all(out[-1], GROUP, 0, 0, tiled=True)
        part, kept = call_planes(partial(adjoint_plane_kernel, scale), tables, came, 12, keeps=True)
        fields = exchange(part)
        fields_image = exchange(call_planes(image_plane_kernel, (lx, ly, xb, yb), [], 4, kept_in=kept))
        sums = []
        for c in both:
            descent[c], part = slabs.call(descent_kernel, c, piece_kinds, ("field", "sum1"), 1, fields)
            sums.append(part)
        sum_d = jnp.sum(sums[0]) + jnp.sum(sums[1])
        sums = []
        for c in both:
            image[c], part = slabs.call(
                image_kernel, c, ("field", "chi") + piece_kinds, ("field", "sum2"), 1,
                descent[c], chi[c], fields_image,
            )
            sums.append(part)
        sum_q = sums[0] + sums[1]
        totals = everyone([sum_d, jnp.sum(sum_q[:, :, 0]), jnp.sum(sum_q[:, :, 1])])
        step = totals[0] / (data_weight * totals[2] + object_weight * totals[1])
        parts = [None, None]
        for c in (1, 0):
            out = slabs.call(
                partial(step_kernel, last),
                c,
                ("scal",) + ("every",) * 4,
                ("every",) * (1 if last else 2) + ("parts",),
                0,
                step.reshape(1, 1), source[c], descent[c], total[c], image[c],
            )
            source[c], parts[c] = out[0], out[-1]
            if not last:
                total[c] = out[1]
        received = swap_halves(parts[1])
        if last:
            sent = payloads(source, shares, per_share, share)
            rounds = deliver(sent[:shares], shares, 0)
            received, *both_sets = lax.optimization_barrier((received, *rounds, *sent[shares:]))
            rounds = both_sets[:shares] + deliver(both_sets[shares:], shares, 1)
        sums = parts[0] + received
        chi_own = bounded(sums[0], sums[1], sums[2], total_sources)
        if not last:
            object_total = everyone([total_sources * jnp.sum(chi_own * chi_own)])[0]
            chi = [chi_own, swap_halves(after(chi_own, object_total))]

    copies = jnp.broadcast_to(chi_own[None], (shares,) + chi_own.shape)
    contrast_new = lax.all_to_all(copies, "src", 0, 0, tiled=True)
    contrast_new = contrast_new.transpose(1, 2, 0, 3, 4).reshape(contrast.shape)
    contrast_sources = assembled(rounds, shares, share, half, contrast_new)
    return contrast_sources, contrast_new


def solution(mesh):
    shares, spaces = mesh.shape["src"], mesh.shape["space"]
    split_mesh = Mesh(mesh.devices.reshape(shares, 2, spaces // 2), ALL)
    space = ("half", "rest")

    return jax.shard_map(
        on_device,
        mesh=split_mesh,
        in_specs=(P(None, None, space, None), P("src", None, space, None), P("src", None)),
        out_specs=(P("src", None, None, space, None), P(None, None, space, None)),
        check_vma=False,
    )
```
